256 devices in a mesh: section: 4 (over x), ex: 16 (over z, core), tp: 4 (over y).
Axes of the slice: x: 4, y: 4, z: 8, core: 2. Of those that a mesh axis runs over, the one named last changes fastest.
Arguments:
- clean_heads: bfloat16 [4, 16, 512, 4096], P('section', 'ex', None, 'tp'), may hold values from -6 to 6
- corrupt_heads: bfloat16 [4, 16, 512, 4096], P('section', 'ex', None, 'tp'), may hold values from -6 to 6
- donors: int32 [512, 16], P('ex'), may hold values from 0 to 15, each once within a row
- senders: int32 [4, 8], P('section', 'tp'), may hold values from 0 to 31, as said below
- out_weight: bfloat16 [4, 4096, 8192], P('section', 'tp', 'ex'), may hold values from -0.1875 to 0.1875
- residual: bfloat16 [4, 16, 512, 8192], P('section', 'ex', None, 'tp'), may hold values from -160 to 160
- norm_gain: bfloat16 [4, 8192], P('section', 'tp'), may hold values from 0.25 to 1.75
- value_weight: bfloat16 [4, 8192, 1024], P('section', 'tp', 'ex'), may hold values from -0.0625 to 0.0625
- clean_values: bfloat16 [4, 16, 512, 1024], P('section', 'ex', None, 'tp'), may hold values from -6 to 6
- queries: bfloat16 [4, 16, 512, 4096], P('section', 'ex', None, 'tp'), may hold values from -120 to 120
- key_vectors: bfloat16 [4, 16, 512, 1024], P('section', 'ex', None, 'tp'), may hold values from -4 to 4
- receivers: int32 [4, 32], P('section', 'tp'), may hold values 0 or 1
Outputs:
- attended: bfloat16 [4, 16, 512, 4096], P('section', 'ex', None, 'tp')
The draws below stay inside these ranges and needn't reach their ends.
Inputs may be any that keep to these rules, and one draw needn't show every extreme that they name: `donors`: each position's row is a permutation of the 16 examples. `senders`: in each section's row, entries j * 2 to (j + 1) * 2 - 1 are distinct heads of j * 8 to (j + 1) * 8 - 1.
All inputs are finite; a program needn't handle non-finite values. No bound on the sum of `receivers` on one device may be relied on, other than what follows from the above.
Results may differ from the reference program's by a relative error of at most 0.012.
Values may be sent and summed in bfloat16 or wider, within the bound.
A program may use at most 128 MiB of HBM per device.

```python
import math
import jax
import jax.numpy as jnp
from jax import lax

D = 8192
KVH = 8
HD = 128
HEADS = 32
GROUP = 4
SEND_DEV = 2
SEQ = 512
SECTIONS = 4
EXAMPLES = 16
SENDERS = 8
QHEADS = 32
N_TP = 4


def pair_draw(key):
    key_one, key_two = jax.random.split(key, 2)
    key_vectors = jnp.clip(jax.random.normal(key_one, (SECTIONS, EXAMPLES, SEQ, KVH, HD), jnp.float32), -4.0, 4.0)
    queries = jnp.clip(jax.random.normal(key_two, (SECTIONS, EXAMPLES, SEQ, KVH, GROUP, HD), jnp.float32), -4.0, 4.0)
    return (queries.reshape(SECTIONS, EXAMPLES, SEQ, KVH * GROUP * HD), key_vectors.reshape(SECTIONS, EXAMPLES, SEQ, KVH * HD))


def draw_queries(key, part):
    return pair_draw(jax.random.fold_in(key, 11))[0].astype(jnp.bfloat16)


def draw_key_vectors(key, part):
    return pair_draw(jax.random.fold_in(key, 11))[1].astype(jnp.bfloat16)


def draw_residual(key, part):
    key_one, key_two = jax.random.split(key, 2)
    shape = (SECTIONS, EXAMPLES, SEQ, D)
    rising = 3.0 ** (jnp.arange(D, dtype=jnp.float32) / D)
    spread = jnp.exp(jax.random.uniform(key_one, (SECTIONS, 1, 1, D), jnp.float32, 0.0, math.log(3.0)))
    sampled = jnp.clip(jax.random.normal(key_two, shape, jnp.float32), -6.0, 6.0)
    return (sampled * rising * spread).astype(jnp.bfloat16)


def draw_senders(key, part):
    blocks = SENDERS // SEND_DEV
    per_block = HEADS // blocks
    stream_keys = jax.random.split(jax.random.fold_in(key, 5), SECTIONS * blocks)
    chosen_heads = jax.vmap(lambda single: jax.random.permutation(single, per_block)[:SEND_DEV])(stream_keys)
    offsets = jnp.arange(SECTIONS * blocks) % blocks * per_block
    return (chosen_heads + offsets[:, None]).reshape(SECTIONS, SENDERS).astype(jnp.int32)


def touch_ends(result, rng, low, top_value):
    longest = result.shape.index(max(result.shape))
    spots = []
    for shift in (0, 1):
        where = [jax.random.randint(jax.random.fold_in(rng, axis), (), 0, length) for axis, length in enumerate(result.shape)]
        where[longest] = (where[longest] + shift) % result.shape[longest]
        spots.append(tuple(where))
    return result.at[spots[0]].set(low).at[spots[1]].set(top_value)


def shard_levels(key, shape, cuts, smallest, largest):
    level = 1.0
    for dim, shards_of in cuts:
        steps = jax.random.uniform(jax.random.fold_in(jax.random.fold_in(key, 6), dim), (shards_of,), jnp.float32, smallest / len(cuts), largest / len(cuts))
        level = level * jnp.repeat(jnp.exp(steps), shape[dim] // shards_of).reshape((-1,) + (1,) * (len(shape) - 1 - dim))
    return level


def normal_values(key, extent, deviation, most, cuts=(), held_as=jnp.bfloat16):
    drawn = jax.random.normal(key, extent, jnp.float32) * deviation
    if len(cuts) > 0:
        drawn = shard_levels(key, extent, cuts, -0.22, 0.18) * drawn
    return jnp.clip(drawn, min=-most, max=most).astype(held_as)


def setup_inputs(seed: int = 0) -> dict:
    seeds = jax.random.split(jax.random.key(seed), 13)
    clean_heads = normal_values(seeds[0], (SECTIONS, EXAMPLES, SEQ, HEADS * HD), 1.0, 6.0, ((0, 4), (1, 16), (3, 4)))
    corrupt_heads = normal_values(seeds[1], (SECTIONS, EXAMPLES, SEQ, HEADS * HD), 1.0, 6.0, ((0, 4), (1, 16), (3, 4)))
    donors = jax.vmap(lambda own: jax.random.permutation(own, EXAMPLES))(jax.random.split(seeds[2], SEQ)).reshape((SEQ, EXAMPLES)).astype(jnp.int32)
    senders = draw_senders(jax.random.fold_in(seeds[12], 71), 0)
    out_weight = normal_values(seeds[4], (SECTIONS, HEADS * HD, D), (SENDERS * HD) ** -0.5, 0.1875, ((0, 4), (1, 4), (2, 16)))
    residual = draw_residual(jax.random.fold_in(seeds[12], 71), 0)
    norm_gain = jnp.clip(1.0 + 0.15 * jax.random.normal(seeds[6], (SECTIONS, D), jnp.float32), 0.25, 1.75).astype(jnp.bfloat16)
    value_weight = normal_values(seeds[7], (SECTIONS, D, KVH * HD), D ** -0.5, 0.0625, ((0, 4), (1, 4), (2, 16)))
    clean_values = normal_values(seeds[8], (SECTIONS, EXAMPLES, SEQ, KVH * HD), 1.0, 6.0, ((0, 4), (1, 16), (3, 4)))
    queries = draw_queries(jax.random.fold_in(seeds[12], 71), 0)
    key_vectors = draw_key_vectors(jax.random.fold_in(seeds[12], 71), 0)
    receivers = touch_ends((jax.random.randint(seeds[11], (SECTIONS, QHEADS), 0, 2) < 1).astype(jnp.int32), jax.random.fold_in(seeds[11], 1), 0, 1)
    return {"clean_heads": clean_heads, "corrupt_heads": corrupt_heads, "donors": donors, "senders": senders, "out_weight": out_weight, "residual": residual, "norm_gain": norm_gain, "value_weight": value_weight, "clean_values": clean_values, "queries": queries, "key_vectors": key_vectors, "receivers": receivers}


def rounded(values):
    return lax.optimization_barrier(values.astype(jnp.bfloat16)).astype(jnp.float32)

def attend(queries, key_vectors, chosen):
    scores = jnp.einsum('etkgd,eukd->ekgtu', queries.astype(jnp.float32), key_vectors.astype(jnp.float32))
    scores = scores * (1.0 / math.sqrt(HD))
    places = jnp.arange(scores.shape[-1])
    causal = places[:, None] >= places[None, :]
    scores = jnp.where(causal, scores, -jnp.inf)
    maxima = lax.optimization_barrier(jnp.max(scores, axis=-1, keepdims=True))
    exponent = jnp.exp(scores - maxima)
    weights = (exponent / lax.optimization_barrier(jnp.sum(exponent, axis=-1, keepdims=True))).astype(jnp.bfloat16)
    return jnp.einsum('ekgtu,eukgd->etkgd', weights.astype(jnp.float32), chosen.astype(jnp.float32))

def reference(clean_heads, corrupt_heads, donors, senders, out_weight, residual, norm_gain, value_weight, clean_values, queries, key_vectors, receivers):
    examples, length = (residual.shape[1], residual.shape[2])
    row_count = examples * length
    width_tp = D // N_TP
    positions = jnp.arange(length)
    carried = jnp.zeros((row_count, D), jnp.float32)
    results = []
    for which_section in range(SECTIONS):
        patched = corrupt_heads[which_section][donors.T, positions[None, :], :]
        difference = patched.astype(jnp.float32) - clean_heads[which_section].astype(jnp.float32)
        difference = difference.reshape(row_count, HEADS, HD)
        head_rows = out_weight[which_section].reshape(HEADS, HD, D)
        increment = jnp.zeros((row_count, D), jnp.float32)
        for which_block in range(N_TP):
            chosen_heads = senders[which_section, which_block * SEND_DEV:(which_block + 1) * SEND_DEV]
            picked = jnp.take(difference, chosen_heads, axis=1).astype(jnp.bfloat16).reshape(row_count, SEND_DEV * HD)
            sender_rows = jnp.take(head_rows, chosen_heads, axis=0).reshape(SEND_DEV * HD, D)
            increment = increment + rounded(jnp.dot(picked, sender_rows, preferred_element_type=jnp.float32))
        carried = carried + increment
        stream = residual[which_section].reshape(row_count, D).astype(jnp.float32) + carried
        scale = lax.rsqrt(lax.optimization_barrier(jnp.mean(stream * stream, axis=-1, keepdims=True)) + 1e-05)
        normed = (stream * scale * norm_gain[which_section].astype(jnp.float32)).astype(jnp.bfloat16)
        values = jnp.zeros((row_count, KVH * HD), jnp.float32)
        for which_block in range(N_TP):
            lower = which_block * width_tp
            values = values + rounded(jnp.dot(normed[:, lower:lower + width_tp], value_weight[which_section, lower:lower + width_tp], preferred_element_type=jnp.float32))
        values = values.astype(jnp.bfloat16).reshape(examples, length, KVH, 1, HD)
        clean_here = clean_values[which_section].reshape(examples, length, KVH, 1, HD)
        receive_flags = receivers[which_section].reshape(KVH, GROUP)
        chosen = jnp.where((receive_flags == 1)[None, None, :, :, None], values, clean_here)
        attended = attend(queries[which_section].reshape(examples, length, KVH, GROUP, HD), key_vectors[which_section].reshape(examples, length, KVH, HD), chosen)
        results.append(attended.reshape(examples, length, KVH * GROUP * HD).astype(jnp.bfloat16))
    return jnp.stack(results)
```

```python
import math

import jax
import jax.numpy as jnp
from jax import lax
from jax.sharding import PartitionSpec as P

D = 8192
HD = 128
GROUP = 4


def pick_columns(array, ids):
    parts = [lax.dynamic_slice_in_dim(array, ids[i] * HD, HD, 1) for i in range(ids.shape[0])]
    return jnp.concatenate(parts, axis=1)


def pick_rows(array, ids):
    parts = [lax.dynamic_slice_in_dim(array, ids[i] * HD, HD, 0) for i in range(ids.shape[0])]
    return jnp.concatenate(parts, axis=0)


def attend(queries, key_vectors, chosen):
    scores = jnp.einsum(
        "etkgd,eukd->ekgtu", queries, key_vectors, preferred_element_type=jnp.float32
    )
    scores = scores * (1.0 / math.sqrt(HD))
    places = jnp.arange(scores.shape[-1])
    causal = places[:, None] >= places[None, :]
    scores = jnp.where(causal, scores, -jnp.inf)
    maxima = jnp.max(scores, axis=-1, keepdims=True)
    exponent = jnp.exp(scores - maxima)
    weights = (exponent / jnp.sum(exponent, axis=-1, keepdims=True)).astype(jnp.bfloat16)
    return jnp.einsum("ekgtu,eukgd->etkgd", weights, chosen, preferred_element_type=jnp.float32)


def chunk_moves(sections, everyone, blocks):
    half = everyone // 2
    moves = []
    for r in range(sections):
        for j in range(everyone):
            for t in range(blocks):
                slot = blocks * r + t
                target_ex = 2 * (slot % half) + slot // half
                source = (r * everyone + j) * blocks + t
                target = ((j % sections) * everyone + target_ex) * blocks + j // sections
                moves.append((source, target))
    return moves


def over_chips(array, everyone):
    same_core = [list(range(c, everyone, 2)) for c in (0, 1)]
    same_chip = [[2 * i, 2 * i + 1] for i in range(everyone // 2)]
    one = lax.all_gather(array, "ex", axis_index_groups=same_core)
    return lax.all_gather(one, "ex", axis_index_groups=same_chip)


def per_device(
    clean_heads,
    corrupt_heads,
    donors,
    senders,
    out_weight,
    residual,
    norm_gain,
    value_weight,
    clean_values,
    queries,
    key_vectors,
    receivers,
):
    length = residual.shape[2]
    heads_here = clean_heads.shape[3] // HD
    sections = lax.axis_size("section")
    everyone = lax.axis_size("ex")
    blocks = lax.axis_size("tp")
    ids = senders[0] - lax.axis_index("tp") * heads_here
    corrupt = pick_columns(corrupt_heads[0, 0], ids)
    clean = pick_columns(clean_heads[0, 0], ids)
    rows = pick_rows(out_weight[0], ids)

    rows = lax.ppermute(rows, ("section", "ex", "tp"), chunk_moves(sections, everyone, blocks))
    weights = over_chips(rows, everyone).reshape(sections, blocks, *rows.shape)
    value_columns = over_chips(value_weight[0].T, everyone)
    value_columns = jnp.swapaxes(value_columns, 0, 1).reshape(-1, value_weight.shape[1])

    gathered = lax.all_to_all(corrupt[None], "ex", split_axis=1, concat_axis=0, tiled=True)
    onehot = (donors[:, :, None] == jnp.arange(everyone)[None, None, :]).astype(jnp.bfloat16)
    patched = jnp.einsum(
        "tef,ftc->etc", onehot, gathered, preferred_element_type=jnp.float32
    ).astype(jnp.bfloat16)
    returned = lax.all_to_all(patched, "ex", split_axis=0, concat_axis=1, tiled=True)[0]
    difference = (returned.astype(jnp.float32) - clean.astype(jnp.float32)).astype(jnp.bfloat16)

    differences = lax.all_gather(difference, ("section", "tp"))
    differences = differences.reshape(sections, blocks, *difference.shape)
    increments = jnp.einsum(
        "rtpk,rtkn->rpn", differences, weights, preferred_element_type=jnp.float32
    )
    running = [increments[0]]
    for r in range(1, sections):
        running.append(running[-1] + increments[r])
    carried = jnp.stack([c.astype(jnp.bfloat16) for c in running])
    carried = lax.all_to_all(carried, "section", 0, 0, tiled=True)
    width = carried.shape[-1]
    stream = residual[0, 0].reshape(length, sections, width).swapaxes(0, 1).astype(
        jnp.float32
    ) + carried.astype(jnp.float32)
    squares = jnp.sum(stream * stream, axis=(0, 2))
    gain = norm_gain[0].reshape(sections, 1, width).astype(jnp.float32)
    scaled = (stream * gain).astype(jnp.bfloat16)
    value_terms = jnp.einsum(
        "spc,nsc->pn",
        scaled,
        value_columns.reshape(-1, sections, width),
        preferred_element_type=jnp.float32,
    ).astype(jnp.bfloat16)
    per_block = value_terms.shape[1] // blocks
    pieces = jnp.moveaxis(value_terms.reshape(length, blocks, per_block), 1, 0)
    pieces = lax.all_to_all(pieces, "tp", 0, 0, tiled=True)
    squares = lax.all_to_all(
        jnp.broadcast_to(squares, (blocks, length)), "tp", 0, 0, tiled=True
    ).sum(axis=0)
    values = jnp.sum(pieces.astype(jnp.float32), axis=0)
    values = (values * lax.rsqrt(squares[:, None] / D + 1e-05)).astype(jnp.bfloat16)

    kv_here = values.shape[-1] // HD
    values = values.reshape(1, length, kv_here, 1, HD)
    clean_here = clean_values[0].reshape(1, length, kv_here, 1, HD)
    receive_flags = receivers[0].reshape(kv_here, GROUP)
    chosen = jnp.where((receive_flags == 1)[None, None, :, :, None], values, clean_here)
    attended = attend(
        queries[0].reshape(1, length, kv_here, GROUP, HD),
        key_vectors[0].reshape(1, length, kv_here, HD),
        chosen,
    )
    return attended.reshape(1, 1, length, -1).astype(jnp.bfloat16)


def solution(mesh):
    return jax.shard_map(
        per_device,
        mesh=mesh,
        in_specs=(
            P("section", "ex", None, "tp"),
            P("section", "ex", None, "tp"),
            P("ex", None),
            P("section", "tp"),
            P("section", "tp", "ex"),
            P("section", "ex", None, "tp"),
            P("section", "tp"),
            P("section", "tp", "ex"),
            P("section", "ex", None, "tp"),
            P("section", "ex", None, "tp"),
            P("section", "ex", None, "tp"),
            P("section", "tp"),
        ),
        out_specs=P("section", "ex", None, "tp"),
        check_vma=False,
    )
```

```python
import math

import jax
import jax.numpy as jnp
from jax import lax
from jax.experimental import pallas as pl
from jax.experimental.pallas import tpu as pltpu
from jax.sharding import PartitionSpec as P

D = 8192
HD = 128
GROUP = 4
SEC = 4
EX = 16
TP = 4
ROWS = 512
HALF = 256
BF = jnp.bfloat16
F32 = jnp.float32
MESH = pl.DeviceIdType.MESH
CHIPS = EX // 2


def dot_nt(a, b):
    return lax.dot_general(a, b, (((1,), (1,)), ((), ())), preferred_element_type=F32)


def remote(src, dst, send, recv, device):
    return pltpu.make_async_remote_copy(
        src_ref=src,
        dst_ref=dst,
        send_sem=send,
        recv_sem=recv,
        device_id=device,
        device_id_type=MESH,
    )


def kernel(
    corrupt,
    clean,
    target,
    weight,
    value_weight,
    flags,
    gain,
    residual_hbm,
    clean_values_hbm,
    queries_hbm,
    keys_hbm,
    out,
    arrived,
    patched,
    returned,
    weights,
    value_weights,
    differences,
    total,
    carried_out,
    carried_in,
    scaled,
    values_out,
    values_in,
    squares_out,
    squares_in,
    values,
    probabilities,
    residual,
    clean_values,
    queries,
    keys,
    local_sem,
    patch_send,
    patch_recv,
    back_send,
    back_recv,
    piece_send,
    piece_recv,
    up_send,
    up_recv,
    down_send,
    down_recv,
    side_send,
    side_recv,
    diff_send,
    diff_recv,
    carry_send,
    carry_recv,
    value_send,
    value_recv,
    square_send,
    square_recv,
):
    sec = lax.axis_index("section")
    ex = lax.axis_index("ex")
    tp = lax.axis_index("tp")
    chip = ex // 2
    core = lax.rem(ex, 2)
    mine = TP * sec + tp
    group = SEC * tp + sec

    loads = [
        pltpu.make_async_copy(queries_hbm, queries, local_sem.at[0]),
        pltpu.make_async_copy(keys_hbm, keys, local_sem.at[1]),
        pltpu.make_async_copy(residual_hbm, residual, local_sem.at[2]),
        pltpu.make_async_copy(clean_values_hbm, clean_values, local_sem.at[3]),
    ]
    for load in loads:
        load.start()

    barrier = pltpu.get_barrier_semaphore()

    @pl.loop(1, EX)
    def _(i):
        pl.semaphore_signal(
            barrier, inc=1, device_id={"ex": lax.rem(ex + i, EX)}, device_id_type=MESH
        )

    def plane_peer(i):
        other = lax.rem(mine + i, EX)
        return other // TP, lax.rem(other, TP)

    @pl.loop(1, EX)
    def _(i):
        s, t = plane_peer(i)
        pl.semaphore_signal(
            barrier, inc=1, device_id={"section": s, "tp": t}, device_id_type=MESH
        )

    pl.semaphore_wait(barrier, 2 * (EX - 1))

    @pl.loop(1, EX)
    def _(i):
        other = lax.rem(ex + i, EX)
        remote(
            corrupt.at[other], arrived.at[ex], patch_send.at[i], patch_recv.at[ex], {"ex": other}
        ).start()

    @pl.loop(1, EX)
    def _(i):
        s, t = plane_peer(i)
        remote(
            weight.at[SEC * t + s],
            weights.at[ex, mine],
            piece_send.at[i],
            piece_recv.at[mine],
            {"section": s, "tp": t},
        ).start()

    arrived[ex] = corrupt[ex]
    weights[ex, mine] = weight[group]
    value_weights[ex] = value_weight[...]

    def ring_start(which, buffer):
        block = buffer.at[ex]
        up = 2 * lax.rem(chip + 1, CHIPS) + core
        down = 2 * lax.rem(chip + CHIPS - 1, CHIPS) + core
        remote(block, block, up_send.at[which, 0], up_recv.at[which, 0], {"ex": up}).start()
        remote(block, block, down_send.at[which, 0], down_recv.at[which, 0], {"ex": down}).start()
        remote(
            block, block, side_send.at[which, 0], side_recv.at[which, 0], {"ex": 2 * chip + 1 - core}
        ).start()

    def ring_relay(which, buffer, step):
        up = 2 * lax.rem(chip + 1, CHIPS) + core
        down = 2 * lax.rem(chip + CHIPS - 1, CHIPS) + core
        side = 2 * chip + 1 - core
        block = buffer.at[2 * lax.rem(chip + CHIPS - step, CHIPS) + core]
        remote(
            block, block, up_send.at[which, step - 1], up_recv.at[which, step - 1], {"ex": up}
        ).wait_recv()
        if step < 4:
            remote(
                block, block, up_send.at[which, step], up_recv.at[which, step], {"ex": up}
            ).start()
        remote(
            block, block, side_send.at[which, step], side_recv.at[which, step], {"ex": side}
        ).start()
        if step < 4:
            block = buffer.at[2 * lax.rem(chip + step, CHIPS) + core]
            remote(
                block,
                block,
                down_send.at[which, step - 1],
                down_recv.at[which, step - 1],
                {"ex": down},
            ).wait_recv()
            if step < 3:
                remote(
                    block, block, down_send.at[which, step], down_recv.at[which, step], {"ex": down}
                ).start()
            remote(
                block,
                block,
                side_send.at[which, 4 + step],
                side_recv.at[which, 4 + step],
                {"ex": side},
            ).start()

    def ring_finish(which, buffer):
        side = 2 * chip + 1 - core
        for step in range(8):
            shift = CHIPS - step if step < 5 else step - 4
            block = buffer.at[2 * lax.rem(chip + shift, CHIPS) + 1 - core]
            remote(
                block, block, side_send.at[which, step], side_recv.at[which, step], {"ex": side}
            ).wait_recv()

    def ring_drain(which, buffer):
        block = buffer.at[ex]
        for step in range(4):
            remote(
                block, block, up_send.at[which, step], up_recv.at[which, step], {"ex": 0}
            ).wait_send()
        for step in range(3):
            remote(
                block, block, down_send.at[which, step], down_recv.at[which, step], {"ex": 0}
            ).wait_send()
        for step in range(8):
            remote(
                block, block, side_send.at[which, step], side_recv.at[which, step], {"ex": 0}
            ).wait_send()

    def softmax(scores):
        exponent = jnp.exp(scores - jnp.max(scores, axis=-1, keepdims=True))
        return (exponent / jnp.sum(exponent, axis=-1, keepdims=True)).astype(BF)

    def weigh_heads(low, high):
        @pl.loop(low, high)
        def _(h):
            lanes = pl.ds(pl.multiple_of(h * HD, HD), HD)
            shared = pl.ds(pl.multiple_of(h // GROUP * HD, HD), HD)
            for half in (0, 1):
                length = HALF * (half + 1)
                scores = dot_nt(
                    queries[half * HALF : (half + 1) * HALF, lanes], keys[:length, shared]
                ) * (1.0 / math.sqrt(HD))
                row = lax.broadcasted_iota(jnp.int32, scores.shape, 0) + half * HALF
                column = lax.broadcasted_iota(jnp.int32, scores.shape, 1)
                scores = jnp.where(row >= column, scores, -jnp.inf)
                probabilities[h, half * HALF : (half + 1) * HALF, :length] = softmax(scores)

    loads[0].wait()
    loads[1].wait()
    weigh_heads(0, 1)

    @pl.loop(1, EX)
    def _(i):
        other = lax.rem(mine + i, EX)
        remote(
            weights.at[ex, other],
            weights.at[ex, other],
            piece_send.at[i],
            piece_recv.at[other],
            {"ex": ex},
        ).wait_recv()

    ring_start(0, weights)

    @pl.loop(1, EX)
    def _(i):
        other = lax.rem(ex + i, EX)
        remote(
            arrived.at[other], arrived.at[other], patch_send.at[i], patch_recv.at[other], {"ex": other}
        ).wait_recv()

    column = lax.broadcasted_iota(jnp.int32, (ROWS, ROWS), 1)
    onehot = (column == target[...]).astype(F32).astype(BF)
    moved = jnp.dot(
        onehot, arrived[...].reshape(ROWS, 2 * HD), preferred_element_type=F32
    ).astype(BF)
    patched[...] = moved.reshape(EX, ROWS // EX, 2 * HD)

    @pl.loop(1, EX)
    def _(i):
        other = lax.rem(ex + i, EX)
        remote(
            patched.at[other], returned.at[ex], back_send.at[i], back_recv.at[ex], {"ex": other}
        ).start()

    returned[ex] = patched[ex]
    weigh_heads(1, 3)

    @pl.loop(1, EX)
    def _(i):
        other = lax.rem(ex + i, EX)
        remote(
            returned.at[other],
            returned.at[other],
            back_send.at[i],
            back_recv.at[other],
            {"ex": other},
        ).wait_recv()

    change = returned[...].reshape(ROWS, 2 * HD).astype(F32) - clean[...].astype(F32)
    differences[0, mine] = change[:HALF].astype(BF)
    differences[1, mine] = change[HALF:].astype(BF)

    def along(axis, half, block, slot):
        here = sec if axis == "section" else tp
        for i in range(1, 4):
            ref = differences.at[half, block]
            remote(
                ref,
                ref,
                diff_send.at[half, slot + i - 1],
                diff_recv.at[half, block],
                {axis: lax.rem(here + i, 4)},
            ).start()

    def difference_wait(half, block):
        ref = differences.at[half, block]
        remote(ref, ref, diff_send.at[half, 0], diff_recv.at[half, block], {"ex": ex}).wait_recv()

    along("tp", 0, mine, 0)
    along("section", 1, mine, 0)
    along("section", 0, mine, 3)
    along("tp", 1, mine, 3)
    ring_relay(0, weights, 1)
    for i in range(1, 4):
        block = TP * sec + lax.rem(tp + i, TP)
        difference_wait(0, block)
        along("section", 0, block, 3 + 3 * i)
        block = TP * lax.rem(sec + i, SEC) + tp
        difference_wait(1, block)
        along("tp", 1, block, 3 + 3 * i)
    ring_relay(0, weights, 2)
    weigh_heads(3, 5)
    ring_relay(0, weights, 3)
    ring_start(1, value_weights)
    weigh_heads(5, 7)
    ring_relay(0, weights, 4)
    ring_finish(0, weights)

    def carry(half):
        @pl.loop(0, SEC)
        def _(r):
            for t in range(TP):
                block = TP * r + t
                first = (block // TP == sec) if half == 0 else (t == tp)
                @pl.when(jnp.logical_not(first))
                def _():
                    difference_wait(half, block)

            term = dot_nt(differences[half, TP * r], weights[:, TP * r].reshape(ROWS, 2 * HD))
            for t in range(1, TP):
                term += dot_nt(
                    differences[half, TP * r + t], weights[:, TP * r + t].reshape(ROWS, 2 * HD)
                )

            @pl.when(r == 0)
            def _():
                total[...] = term

            @pl.when(r > 0)
            def _():
                total[...] += term

            rounded = total[...].astype(BF)
            for t in range(TP):
                carried_out[half, r, t] = rounded[:, t * HD : (t + 1) * HD]
                here = jnp.logical_and(r == sec, t == tp)

                @pl.when(here)
                def _():
                    carried_in[half, group] = carried_out[half, r, t]

                @pl.when(jnp.logical_not(here))
                def _():
                    remote(
                        carried_out.at[half, r, t],
                        carried_in.at[half, group],
                        carry_send.at[half, TP * r + t],
                        carry_recv.at[half, group],
                        {"section": r, "tp": t},
                    ).start()

    carry(0)
    ring_relay(1, value_weights, 1)
    carry(1)
    ring_relay(1, value_weights, 2)
    weigh_heads(7, 8)
    ring_relay(1, value_weights, 3)
    ring_relay(1, value_weights, 4)
    ring_finish(1, value_weights)
    loads[2].wait()
    loads[3].wait()

    source = lax.broadcasted_iota(jnp.int32, (ROWS, ROWS), 0)
    column = lax.broadcasted_iota(jnp.int32, (ROWS, ROWS), 1)
    place = source // 32 % 4 * 128 + source // 128 * 32 + source % 32
    order = (place == column).astype(F32).astype(BF)

    def finish_stream(half):
        rows = slice(half * HALF, (half + 1) * HALF)

        @pl.loop(1, EX)
        def _(i):
            other = lax.rem(group + i, EX)
            remote(
                carried_in.at[half, other],
                carried_in.at[half, other],
                carry_send.at[half, 0],
                carry_recv.at[half, other],
                {"ex": ex},
            ).wait_recv()

        square = jnp.zeros((HALF, HD), F32)
        for g in range(4):
            pieces = jnp.concatenate([carried_in[half, 4 * g + q] for q in range(4)], axis=1)
            ordered = jnp.dot(pieces, order, preferred_element_type=F32)
            for j in range(4):
                lanes = slice(j * ROWS + g * HD, j * ROWS + (g + 1) * HD)
                stream = residual[rows, lanes].astype(F32) + ordered[:, j * HD : (j + 1) * HD]
                square += stream * stream
                scaled[rows, lanes] = (stream * gain[:, lanes].astype(F32)).astype(BF)
        sums = jnp.broadcast_to(jnp.sum(square, axis=1, keepdims=True), (HALF, HD))
        squares_out[half] = jnp.transpose(sums)[:8]
        squares_in[half, tp] = squares_out[half]
        for i in range(1, TP):
            other = lax.rem(tp + i, TP)
            remote(
                squares_out.at[half],
                squares_in.at[half, tp],
                square_send.at[half, i],
                square_recv.at[half, tp],
                {"tp": other},
            ).start()

        @pl.loop(1, TP + 1)
        def _(i):
            other = lax.rem(tp + i, TP)
            columns = value_weights[pl.ds(4 * other, 4)].reshape(2 * HD, SEC * ROWS)
            values_out[half, other] = dot_nt(scaled[rows, :], columns).astype(BF)

            @pl.when(i < TP)
            def _():
                remote(
                    values_out.at[half, other],
                    values_in.at[half, tp],
                    value_send.at[half, other],
                    value_recv.at[half, tp],
                    {"tp": other},
                ).start()

        values_in[half, tp] = values_out[half, tp]

    def attend(half):
        rows = slice(half * HALF, (half + 1) * HALF)
        for i in range(1, TP):
            other = lax.rem(tp + i, TP)
            remote(
                values_in.at[half, other],
                values_in.at[half, other],
                value_send.at[half, 0],
                value_recv.at[half, other],
                {"ex": ex},
            ).wait_recv()
            remote(
                squares_in.at[half, other],
                squares_in.at[half, other],
                square_send.at[half, 0],
                square_recv.at[half, other],
                {"ex": ex},
            ).wait_recv()
        squares = (squares_in[half, 0] + squares_in[half, 1]) + (
            squares_in[half, 2] + squares_in[half, 3]
        )
        scale = lax.rsqrt(squares / D + 1e-05)
        scale = jnp.transpose(jnp.concatenate([scale] * 16, axis=0))
        for g in (0, 1):
            lanes = slice(g * HD, (g + 1) * HD)
            summed = values_in[half, 0, :, lanes].astype(F32)
            for t in range(1, TP):
                summed += values_in[half, t, :, lanes].astype(F32)
            values[rows, lanes] = (summed * scale).astype(BF)
        length = HALF * (half + 1)

        @pl.loop(0, 2 * GROUP)
        def _(h):
            shared = pl.ds(pl.multiple_of(h // GROUP * HD, HD), HD)
            flag = jnp.broadcast_to(flags[pl.ds(h, 1), :], (length, HD)) == 1
            chosen = jnp.where(
                flag,
                values[:length, shared].astype(F32),
                clean_values[:length, shared].astype(F32),
            ).astype(BF)
            out[rows, pl.ds(pl.multiple_of(h * HD, HD), HD)] = jnp.dot(
                probabilities[h, rows, :length], chosen, preferred_element_type=F32
            ).astype(BF)

    finish_stream(0)
    finish_stream(1)
    attend(0)
    attend(1)

    @pl.loop(1, EX)
    def _(i):
        remote(corrupt.at[0], arrived.at[0], patch_send.at[i], patch_recv.at[0], {"ex": 0}).wait_send()
        remote(patched.at[0], returned.at[0], back_send.at[i], back_recv.at[0], {"ex": 0}).wait_send()
        remote(
            weight.at[0], weights.at[0, 0], piece_send.at[i], piece_recv.at[0], {"ex": 0}
        ).wait_send()

    ring_drain(0, weights)
    ring_drain(1, value_weights)
    for half in (0, 1):

        @pl.loop(0, EX - 1)
        def _(i):
            ref = differences.at[half, 0]
            remote(ref, ref, diff_send.at[half, i], diff_recv.at[half, 0], {"ex": 0}).wait_send()

        @pl.loop(1, EX)
        def _(i):
            other = lax.rem(mine + i, EX)
            remote(
                carried_out.at[half, 0, 0],
                carried_in.at[half, 0],
                carry_send.at[half, other],
                carry_recv.at[half, 0],
                {"ex": 0},
            ).wait_send()

        for i in range(1, TP):
            other = lax.rem(tp + i, TP)
            remote(
                values_out.at[half, 0],
                values_in.at[half, 0],
                value_send.at[half, other],
                value_recv.at[half, 0],
                {"ex": 0},
            ).wait_send()
            remote(
                squares_out.at[half],
                squares_in.at[half, 0],
                square_send.at[half, i],
                square_recv.at[half, 0],
                {"ex": 0},
            ).wait_send()


def pick_columns(array, ids):
    parts = [lax.dynamic_slice_in_dim(array, ids[i] * HD, HD, 1) for i in range(ids.shape[0])]
    return jnp.concatenate(parts, axis=1)


def pick_rows(array, ids):
    parts = [lax.dynamic_slice_in_dim(array, ids[i] * HD, HD, 0) for i in range(ids.shape[0])]
    return jnp.concatenate(parts, axis=0)


def per_device(
    clean_heads,
    corrupt_heads,
    donors,
    senders,
    out_weight,
    residual,
    norm_gain,
    value_weight,
    clean_values,
    queries,
    key_vectors,
    receivers,
):
    heads_here = clean_heads.shape[3] // HD
    ids = senders[0] - lax.axis_index("tp") * heads_here
    corrupt = pick_columns(corrupt_heads[0, 0], ids).reshape(EX, ROWS // EX, 2 * HD)
    clean = pick_columns(clean_heads[0, 0], ids)
    weight = pick_rows(out_weight[0], ids).T.reshape(EX, ROWS // EX, 2 * HD)
    block = ROWS // EX
    target = (donors.T * block + jnp.arange(block, dtype=jnp.int32)[None, :]).reshape(ROWS, 1)
    flags = jnp.broadcast_to(receivers[0][:, None], (2 * GROUP, HD))
    dma = pltpu.SemaphoreType.DMA
    vmem = pl.BlockSpec(memory_space=pltpu.VMEM)
    hbm = pl.BlockSpec(memory_space=pl.ANY)
    attended = pl.pallas_call(
        kernel,
        out_shape=jax.ShapeDtypeStruct((ROWS, 2 * GROUP * HD), BF),
        in_specs=[vmem] * 7 + [hbm] * 4,
        out_specs=vmem,
        scratch_shapes=[
            pltpu.VMEM((EX, 32, 2 * HD), BF),
            pltpu.VMEM((EX, 32, 2 * HD), BF),
            pltpu.VMEM((EX, 32, 2 * HD), BF),
            pltpu.VMEM((EX, EX, 32, 2 * HD), BF),
            pltpu.VMEM((EX, 64, SEC * ROWS), BF),
            pltpu.VMEM((2, EX, HALF, 2 * HD), BF),
            pltpu.VMEM((HALF, ROWS), F32),
            pltpu.VMEM((2, SEC, TP, HALF, HD), BF),
            pltpu.VMEM((2, EX, HALF, HD), BF),
            pltpu.VMEM((ROWS, SEC * ROWS), BF),
            pltpu.VMEM((2, TP, HALF, 2 * HD), BF),
            pltpu.VMEM((2, TP, HALF, 2 * HD), BF),
            pltpu.VMEM((2, 8, HALF), F32),
            pltpu.VMEM((2, TP, 8, HALF), F32),
            pltpu.VMEM((ROWS, 2 * HD), BF),
            pltpu.VMEM((2 * GROUP, ROWS, ROWS), BF),
            pltpu.VMEM((ROWS, SEC * ROWS), BF),
            pltpu.VMEM((ROWS, 2 * HD), BF),
            pltpu.VMEM((ROWS, 2 * GROUP * HD), BF),
            pltpu.VMEM((ROWS, 2 * HD), BF),
            dma((4,)),
            dma((EX,)),
            dma((EX,)),
            dma((EX,)),
            dma((EX,)),
            dma((EX,)),
            dma((EX,)),
            dma((2, 4)),
            dma((2, 4)),
            dma((2, 3)),
            dma((2, 3)),
            dma((2, 8)),
            dma((2, 8)),
            dma((2, EX - 1)),
            dma((2, EX)),
            dma((2, EX)),
            dma((2, EX)),
            dma((2, TP)),
            dma((2, TP)),
            dma((2, TP)),
            dma((2, TP)),
        ],
        compiler_params=pltpu.CompilerParams(
            collective_id=0, has_side_effects=True, vmem_limit_bytes=56 * 2**20
        ),
    )(
        corrupt,
        clean,
        target,
        weight,
        value_weight[0].T,
        flags,
        norm_gain,
        residual[0, 0],
        clean_values[0, 0],
        queries[0, 0],
        key_vectors[0, 0],
    )
    return attended.reshape(1, 1, ROWS, -1)


def solution(mesh):
    return jax.shard_map(
        per_device,
        mesh=mesh,
        in_specs=(
            P("section", "ex", None, "tp"),
            P("section", "ex", None, "tp"),
            P("ex", None),
            P("section", "tp"),
            P("section", "tp", "ex"),
            P("section", "ex", None, "tp"),
            P("section", "tp"),
            P("section", "tp", "ex"),
            P("section", "ex", None, "tp"),
            P("section", "ex", None, "tp"),
            P("section", "ex", None, "tp"),
            P("section", "tp"),
        ),
        out_specs=P("section", "ex", None, "tp"),
        check_vma=False,
    )
```

```python
import math

import jax
import jax.numpy as jnp
from jax import lax
from jax.experimental import pallas as pl
from jax.experimental.pallas import tpu as pltpu
from jax.sharding import PartitionSpec as P

D = 8192
HD = 128
GROUP = 4
SEC = 4
EX = 16
TP = 4
ROWS = 512
HALF = 256
BF = jnp.bfloat16
F32 = jnp.float32
MESH = pl.DeviceIdType.MESH
CHIPS = EX // 2


def dot_nt(a, b):
    return lax.dot_general(a, b, (((1,), (1,)), ((), ())), preferred_element_type=F32)


def remote(src, dst, send, recv, device):
    return pltpu.make_async_remote_copy(
        src_ref=src,
        dst_ref=dst,
        send_sem=send,
        recv_sem=recv,
        device_id=device,
        device_id_type=MESH,
    )


def kernel(
    senders,
    receivers,
    donors,
    gain,
    corrupt_hbm,
    clean_hbm,
    weight_hbm,
    value_weight_hbm,
    residual_hbm,
    clean_values_hbm,
    queries_hbm,
    keys_hbm,
    out,
    arrived,
    patched,
    returned,
    weights,
    value_weights,
    differences,
    total,
    carried_out,
    carried_in,
    scaled,
    values_out,
    values_in,
    squares_out,
    squares_in,
    values,
    probabilities,
    residual,
    clean_values,
    queries,
    keys,
    corrupt_all,
    clean_all,
    weight_all,
    corrupt,
    clean,
    weight,
    flags,
    local_sem,
    patch_send,
    patch_recv,
    back_send,
    back_recv,
    piece_send,
    piece_recv,
    up_send,
    up_recv,
    down_send,
    down_recv,
    side_send,
    side_recv,
    diff_send,
    diff_recv,
    carry_send,
    carry_recv,
    value_send,
    value_recv,
    square_send,
    square_recv,
):
    sec = lax.axis_index("section")
    ex = lax.axis_index("ex")
    tp = lax.axis_index("tp")
    chip = ex // 2
    core = lax.rem(ex, 2)
    mine = TP * sec + tp
    group = SEC * tp + sec

    loads = [
        pltpu.make_async_copy(queries_hbm, queries, local_sem.at[0]),
        pltpu.make_async_copy(keys_hbm, keys, local_sem.at[1]),
        pltpu.make_async_copy(residual_hbm, residual, local_sem.at[2]),
        pltpu.make_async_copy(clean_values_hbm, clean_values, local_sem.at[3]),
        pltpu.make_async_copy(clean_hbm, clean_all, local_sem.at[4]),
    ]
    first_loads = [
        pltpu.make_async_copy(corrupt_hbm, corrupt_all, local_sem.at[5]),
        pltpu.make_async_copy(weight_hbm, weight_all, local_sem.at[6]),
        pltpu.make_async_copy(value_weight_hbm, value_weights.at[ex], local_sem.at[7]),
    ]
    for load in first_loads:
        load.start()

    barrier = pltpu.get_barrier_semaphore()

    @pl.loop(1, EX)
    def _(i):
        pl.semaphore_signal(
            barrier, inc=1, device_id={"ex": lax.rem(ex + i, EX)}, device_id_type=MESH
        )

    def plane_peer(i):
        other = lax.rem(mine + i, EX)
        return other // TP, lax.rem(other, TP)

    @pl.loop(1, EX)
    def _(i):
        s, t = plane_peer(i)
        pl.semaphore_signal(
            barrier, inc=1, device_id={"section": s, "tp": t}, device_id_type=MESH
        )

    heads_here = 2 * GROUP
    feature = lax.broadcasted_iota(jnp.int32, (heads_here * HD, HD), 0)
    lane = lax.broadcasted_iota(jnp.int32, (heads_here * HD, HD), 1)
    picks = []
    for i in (0, 1):
        head = senders[:, i : i + 1] - heads_here * tp
        picks.append((feature - lane == head * HD).astype(F32).astype(BF))
    pick = jnp.concatenate(picks, axis=1)
    first_loads[0].wait()
    corrupt[...] = (
        jnp.dot(corrupt_all[...], pick, preferred_element_type=F32)
        .astype(BF)
        .reshape(EX, ROWS // EX, 2 * HD)
    )

    pl.semaphore_wait(barrier, 2 * (EX - 1))

    @pl.loop(1, EX)
    def _(i):
        other = lax.rem(ex + i, EX)
        remote(
            corrupt.at[other], arrived.at[ex], patch_send.at[i], patch_recv.at[ex], {"ex": other}
        ).start()

    arrived[ex] = corrupt[ex]
    first_loads[1].wait()
    weight[...] = (
        lax.dot_general(
            weight_all[...], pick, (((0,), (0,)), ((), ())), preferred_element_type=F32
        )
        .astype(BF)
        .reshape(EX, ROWS // EX, 2 * HD)
    )

    @pl.loop(1, EX)
    def _(i):
        s, t = plane_peer(i)
        remote(
            weight.at[SEC * t + s],
            weights.at[ex, mine],
            piece_send.at[i],
            piece_recv.at[mine],
            {"section": s, "tp": t},
        ).start()

    weights[ex, mine] = weight[group]
    for load in loads:
        load.start()
    first_loads[2].wait()

    def ring_start(which, buffer):
        block = buffer.at[ex]
        up = 2 * lax.rem(chip + 1, CHIPS) + core
        down = 2 * lax.rem(chip + CHIPS - 1, CHIPS) + core
        remote(block, block, up_send.at[which, 0], up_recv.at[which, 0], {"ex": up}).start()
        remote(block, block, down_send.at[which, 0], down_recv.at[which, 0], {"ex": down}).start()
        remote(
            block, block, side_send.at[which, 0], side_recv.at[which, 0], {"ex": 2 * chip + 1 - core}
        ).start()

    def ring_relay(which, buffer, step):
        up = 2 * lax.rem(chip + 1, CHIPS) + core
        down = 2 * lax.rem(chip + CHIPS - 1, CHIPS) + core
        side = 2 * chip + 1 - core
        block = buffer.at[2 * lax.rem(chip + CHIPS - step, CHIPS) + core]
        remote(
            block, block, up_send.at[which, step - 1], up_recv.at[which, step - 1], {"ex": up}
        ).wait_recv()
        if step < 4:
            remote(
                block, block, up_send.at[which, step], up_recv.at[which, step], {"ex": up}
            ).start()
        remote(
            block, block, side_send.at[which, step], side_recv.at[which, step], {"ex": side}
        ).start()
        if step < 4:
            block = buffer.at[2 * lax.rem(chip + step, CHIPS) + core]
            remote(
                block,
                block,
                down_send.at[which, step - 1],
                down_recv.at[which, step - 1],
                {"ex": down},
            ).wait_recv()
            if step < 3:
                remote(
                    block, block, down_send.at[which, step], down_recv.at[which, step], {"ex": down}
                ).start()
            remote(
                block,
                block,
                side_send.at[which, 4 + step],
                side_recv.at[which, 4 + step],
                {"ex": side},
            ).start()

    def ring_finish(which, buffer):
        side = 2 * chip + 1 - core
        for step in range(8):
            shift = CHIPS - step if step < 5 else step - 4
            block = buffer.at[2 * lax.rem(chip + shift, CHIPS) + 1 - core]
            remote(
                block, block, side_send.at[which, step], side_recv.at[which, step], {"ex": side}
            ).wait_recv()

    def ring_drain(which, buffer):
        block = buffer.at[ex]
        for step in range(4):
            remote(
                block, block, up_send.at[which, step], up_recv.at[which, step], {"ex": 0}
            ).wait_send()
        for step in range(3):
            remote(
                block, block, down_send.at[which, step], down_recv.at[which, step], {"ex": 0}
            ).wait_send()
        for step in range(8):
            remote(
                block, block, side_send.at[which, step], side_recv.at[which, step], {"ex": 0}
            ).wait_send()

    def softmax(scores):
        exponent = jnp.exp(scores - jnp.max(scores, axis=-1, keepdims=True))
        return (exponent / jnp.sum(exponent, axis=-1, keepdims=True)).astype(BF)

    def weigh_heads(low, high):
        @pl.loop(low, high)
        def _(h):
            lanes = pl.ds(pl.multiple_of(h * HD, HD), HD)
            shared = pl.ds(pl.multiple_of(h // GROUP * HD, HD), HD)
            for half in (0, 1):
                length = HALF * (half + 1)
                scores = dot_nt(
                    queries[half * HALF : (half + 1) * HALF, lanes], keys[:length, shared]
                ) * (1.0 / math.sqrt(HD))
                row = lax.broadcasted_iota(jnp.int32, scores.shape, 0) + half * HALF
                column = lax.broadcasted_iota(jnp.int32, scores.shape, 1)
                scores = jnp.where(row >= column, scores, -jnp.inf)
                probabilities[h, half * HALF : (half + 1) * HALF, :length] = softmax(scores)

    loads[0].wait()
    loads[1].wait()
    weigh_heads(0, 1)

    block = ROWS // EX
    same = lax.broadcasted_iota(jnp.int32, (block, block), 0) == lax.broadcasted_iota(
        jnp.int32, (block, block), 1
    )
    donor = dot_nt(same.astype(F32).astype(BF), donors[...].astype(F32).astype(BF))
    row = lax.broadcasted_iota(jnp.int32, (block, ROWS), 0)
    column = lax.broadcasted_iota(jnp.int32, (block, ROWS), 1)
    offset = (column - row).astype(F32)
    onehot = jnp.concatenate(
        [
            (offset == donor[:, e : e + 1] * block).astype(F32).astype(BF)
            for e in range(EX)
        ],
        axis=0,
    )
    loads[4].wait()
    clean[...] = jnp.dot(clean_all[...], pick, preferred_element_type=F32).astype(BF)
    for h in range(heads_here):
        flags[h : h + 1, :] = jnp.broadcast_to(receivers[:, h : h + 1], (1, HD))

    @pl.loop(1, EX)
    def _(i):
        other = lax.rem(mine + i, EX)
        remote(
            weights.at[ex, other],
            weights.at[ex, other],
            piece_send.at[i],
            piece_recv.at[other],
            {"ex": ex},
        ).wait_recv()

    ring_start(0, weights)

    @pl.loop(1, EX)
    def _(i):
        other = lax.rem(ex + i, EX)
        remote(
            arrived.at[other], arrived.at[other], patch_send.at[i], patch_recv.at[other], {"ex": other}
        ).wait_recv()

    moved = jnp.dot(
        onehot, arrived[...].reshape(ROWS, 2 * HD), preferred_element_type=F32
    ).astype(BF)
    patched[...] = moved.reshape(EX, ROWS // EX, 2 * HD)

    @pl.loop(1, EX)
    def _(i):
        other = lax.rem(ex + i, EX)
        remote(
            patched.at[other], returned.at[ex], back_send.at[i], back_recv.at[ex], {"ex": other}
        ).start()

    returned[ex] = patched[ex]
    weigh_heads(1, 3)

    @pl.loop(1, EX)
    def _(i):
        other = lax.rem(ex + i, EX)
        remote(
            returned.at[other],
            returned.at[other],
            back_send.at[i],
            back_recv.at[other],
            {"ex": other},
        ).wait_recv()

    change = returned[...].reshape(ROWS, 2 * HD).astype(F32) - clean[...].astype(F32)
    differences[0, mine] = change[:HALF].astype(BF)
    differences[1, mine] = change[HALF:].astype(BF)

    def along(axis, half, block, slot):
        here = sec if axis == "section" else tp
        for i in range(1, 4):
            ref = differences.at[half, block]
            remote(
                ref,
                ref,
                diff_send.at[half, slot + i - 1],
                diff_recv.at[half, block],
                {axis: lax.rem(here + i, 4)},
            ).start()

    def difference_wait(half, block):
        ref = differences.at[half, block]
        remote(ref, ref, diff_send.at[half, 0], diff_recv.at[half, block], {"ex": ex}).wait_recv()

    along("tp", 0, mine, 0)
    along("section", 1, mine, 0)
    along("section", 0, mine, 3)
    along("tp", 1, mine, 3)
    ring_relay(0, weights, 1)
    for i in range(1, 4):
        block = TP * sec + lax.rem(tp + i, TP)
        difference_wait(0, block)
        along("section", 0, block, 3 + 3 * i)
        block = TP * lax.rem(sec + i, SEC) + tp
        difference_wait(1, block)
        along("tp", 1, block, 3 + 3 * i)
    ring_relay(0, weights, 2)
    weigh_heads(3, 5)
    ring_relay(0, weights, 3)
    ring_start(1, value_weights)
    weigh_heads(5, 7)
    ring_relay(0, weights, 4)
    ring_finish(0, weights)

    def carry(half):
        @pl.loop(0, SEC)
        def _(r):
            for t in range(TP):
                block = TP * r + t
                first = (block // TP == sec) if half == 0 else (t == tp)
                @pl.when(jnp.logical_not(first))
                def _():
                    difference_wait(half, block)

            term = dot_nt(differences[half, TP * r], weights[:, TP * r].reshape(ROWS, 2 * HD))
            for t in range(1, TP):
                term += dot_nt(
                    differences[half, TP * r + t], weights[:, TP * r + t].reshape(ROWS, 2 * HD)
                )

            @pl.when(r == 0)
            def _():
                total[...] = term

            @pl.when(r > 0)
            def _():
                total[...] += term

            rounded = total[...].astype(BF)
            for t in range(TP):
                carried_out[half, r, t] = rounded[:, t * HD : (t + 1) * HD]
                here = jnp.logical_and(r == sec, t == tp)

                @pl.when(here)
                def _():
                    carried_in[half, group] = carried_out[half, r, t]

                @pl.when(jnp.logical_not(here))
                def _():
                    remote(
                        carried_out.at[half, r, t],
                        carried_in.at[half, group],
                        carry_send.at[half, TP * r + t],
                        carry_recv.at[half, group],
                        {"section": r, "tp": t},
                    ).start()

    carry(0)
    ring_relay(1, value_weights, 1)
    carry(1)
    ring_relay(1, value_weights, 2)
    weigh_heads(7, 8)
    ring_relay(1, value_weights, 3)
    ring_relay(1, value_weights, 4)
    ring_finish(1, value_weights)
    loads[2].wait()
    loads[3].wait()

    source = lax.broadcasted_iota(jnp.int32, (ROWS, ROWS), 0)
    column = lax.broadcasted_iota(jnp.int32, (ROWS, ROWS), 1)
    place = source // 32 % 4 * 128 + source // 128 * 32 + source % 32
    order = (place == column).astype(F32).astype(BF)

    def finish_stream(half):
        rows = slice(half * HALF, (half + 1) * HALF)

        @pl.loop(1, EX)
        def _(i):
            other = lax.rem(group + i, EX)
            remote(
                carried_in.at[half, other],
                carried_in.at[half, other],
                carry_send.at[half, 0],
                carry_recv.at[half, other],
                {"ex": ex},
            ).wait_recv()

        square = jnp.zeros((HALF, HD), F32)
        for g in range(4):
            pieces = jnp.concatenate([carried_in[half, 4 * g + q] for q in range(4)], axis=1)
            ordered = jnp.dot(pieces, order, preferred_element_type=F32)
            for j in range(4):
                lanes = slice(j * ROWS + g * HD, j * ROWS + (g + 1) * HD)
                stream = residual[rows, lanes].astype(F32) + ordered[:, j * HD : (j + 1) * HD]
                square += stream * stream
                scaled[rows, lanes] = (stream * gain[:, lanes].astype(F32)).astype(BF)
        sums = jnp.broadcast_to(jnp.sum(square, axis=1, keepdims=True), (HALF, HD))
        squares_out[half] = jnp.transpose(sums)[:8]
        squares_in[half, tp] = squares_out[half]
        for i in range(1, TP):
            other = lax.rem(tp + i, TP)
            remote(
                squares_out.at[half],
                squares_in.at[half, tp],
                square_send.at[half, i],
                square_recv.at[half, tp],
                {"tp": other},
            ).start()

        @pl.loop(1, TP + 1)
        def _(i):
            other = lax.rem(tp + i, TP)
            columns = value_weights[pl.ds(4 * other, 4)].reshape(2 * HD, SEC * ROWS)
            values_out[half, other] = dot_nt(scaled[rows, :], columns).astype(BF)

            @pl.when(i < TP)
            def _():
                remote(
                    values_out.at[half, other],
                    values_in.at[half, tp],
                    value_send.at[half, other],
                    value_recv.at[half, tp],
                    {"tp": other},
                ).start()

        values_in[half, tp] = values_out[half, tp]

    def attend(half):
        rows = slice(half * HALF, (half + 1) * HALF)
        for i in range(1, TP):
            other = lax.rem(tp + i, TP)
            remote(
                values_in.at[half, other],
                values_in.at[half, other],
                value_send.at[half, 0],
                value_recv.at[half, other],
                {"ex": ex},
            ).wait_recv()
            remote(
                squares_in.at[half, other],
                squares_in.at[half, other],
                square_send.at[half, 0],
                square_recv.at[half, other],
                {"ex": ex},
            ).wait_recv()
        squares = (squares_in[half, 0] + squares_in[half, 1]) + (
            squares_in[half, 2] + squares_in[half, 3]
        )
        scale = lax.rsqrt(squares / D + 1e-05)
        scale = jnp.transpose(jnp.concatenate([scale] * 16, axis=0))
        for g in (0, 1):
            lanes = slice(g * HD, (g + 1) * HD)
            summed = values_in[half, 0, :, lanes].astype(F32)
            for t in range(1, TP):
                summed += values_in[half, t, :, lanes].astype(F32)
            values[rows, lanes] = (summed * scale).astype(BF)
        length = HALF * (half + 1)

        @pl.loop(0, 2 * GROUP)
        def _(h):
            shared = pl.ds(pl.multiple_of(h // GROUP * HD, HD), HD)
            flag = jnp.broadcast_to(flags[pl.ds(h, 1), :], (length, HD)) == 1
            chosen = jnp.where(
                flag,
                values[:length, shared].astype(F32),
                clean_values[:length, shared].astype(F32),
            ).astype(BF)
            out[rows, pl.ds(pl.multiple_of(h * HD, HD), HD)] = jnp.dot(
                probabilities[h, rows, :length], chosen, preferred_element_type=F32
            ).astype(BF)

    finish_stream(0)
    finish_stream(1)
    attend(0)
    attend(1)

    @pl.loop(1, EX)
    def _(i):
        remote(corrupt.at[0], arrived.at[0], patch_send.at[i], patch_recv.at[0], {"ex": 0}).wait_send()
        remote(patched.at[0], returned.at[0], back_send.at[i], back_recv.at[0], {"ex": 0}).wait_send()
        remote(
            weight.at[0], weights.at[0, 0], piece_send.at[i], piece_recv.at[0], {"ex": 0}
        ).wait_send()

    ring_drain(0, weights)
    ring_drain(1, value_weights)
    for half in (0, 1):

        @pl.loop(0, EX - 1)
        def _(i):
            ref = differences.at[half, 0]
            remote(ref, ref, diff_send.at[half, i], diff_recv.at[half, 0], {"ex": 0}).wait_send()

        @pl.loop(1, EX)
        def _(i):
            other = lax.rem(mine + i, EX)
            remote(
                carried_out.at[half, 0, 0],
                carried_in.at[half, 0],
                carry_send.at[half, other],
                carry_recv.at[half, 0],
                {"ex": 0},
            ).wait_send()

        for i in range(1, TP):
            other = lax.rem(tp + i, TP)
            remote(
                values_out.at[half, 0],
                values_in.at[half, 0],
                value_send.at[half, other],
                value_recv.at[half, 0],
                {"ex": 0},
            ).wait_send()
            remote(
                squares_out.at[half],
                squares_in.at[half, 0],
                square_send.at[half, i],
                square_recv.at[half, 0],
                {"ex": 0},
            ).wait_send()


def per_device(
    clean_heads,
    corrupt_heads,
    donors,
    senders,
    out_weight,
    residual,
    norm_gain,
    value_weight,
    clean_values,
    queries,
    key_vectors,
    receivers,
):
    dma = pltpu.SemaphoreType.DMA
    vmem = pl.BlockSpec(memory_space=pltpu.VMEM)
    hbm = pl.BlockSpec(memory_space=pl.ANY)
    attended = pl.pallas_call(
        kernel,
        out_shape=jax.ShapeDtypeStruct((ROWS, 2 * GROUP * HD), BF),
        in_specs=[vmem] * 4 + [hbm] * 8,
        out_specs=vmem,
        scratch_shapes=[
            pltpu.VMEM((EX, 32, 2 * HD), BF),
            pltpu.VMEM((EX, 32, 2 * HD), BF),
            pltpu.VMEM((EX, 32, 2 * HD), BF),
            pltpu.VMEM((EX, EX, 32, 2 * HD), BF),
            pltpu.VMEM((EX, 64, SEC * ROWS), BF),
            pltpu.VMEM((2, EX, HALF, 2 * HD), BF),
            pltpu.VMEM((HALF, ROWS), F32),
            pltpu.VMEM((2, SEC, TP, HALF, HD), BF),
            pltpu.VMEM((2, EX, HALF, HD), BF),
            pltpu.VMEM((ROWS, SEC * ROWS), BF),
            pltpu.VMEM((2, TP, HALF, 2 * HD), BF),
            pltpu.VMEM((2, TP, HALF, 2 * HD), BF),
            pltpu.VMEM((2, 8, HALF), F32),
            pltpu.VMEM((2, TP, 8, HALF), F32),
            pltpu.VMEM((ROWS, 2 * HD), BF),
            pltpu.VMEM((2 * GROUP, ROWS, ROWS), BF),
            pltpu.VMEM((ROWS, SEC * ROWS), BF),
            pltpu.VMEM((ROWS, 2 * HD), BF),
            pltpu.VMEM((ROWS, 2 * GROUP * HD), BF),
            pltpu.VMEM((ROWS, 2 * HD), BF),
            pltpu.VMEM((ROWS, 8 * HD), BF),
            pltpu.VMEM((ROWS, 8 * HD), BF),
            pltpu.VMEM((8 * HD, ROWS), BF),
            pltpu.VMEM((EX, 32, 2 * HD), BF),
            pltpu.VMEM((ROWS, 2 * HD), BF),
            pltpu.VMEM((EX, 32, 2 * HD), BF),
            pltpu.VMEM((2 * GROUP, HD), jnp.int32),
            dma((8,)),
            dma((EX,)),
            dma((EX,)),
            dma((EX,)),
            dma((EX,)),
            dma((EX,)),
            dma((EX,)),
            dma((2, 4)),
            dma((2, 4)),
            dma((2, 3)),
            dma((2, 3)),
            dma((2, 8)),
            dma((2, 8)),
            dma((2, EX - 1)),
            dma((2, EX)),
            dma((2, EX)),
            dma((2, EX)),
            dma((2, TP)),
            dma((2, TP)),
            dma((2, TP)),
            dma((2, TP)),
        ],
        compiler_params=pltpu.CompilerParams(
            collective_id=0, has_side_effects=True, vmem_limit_bytes=56 * 2**20
        ),
    )(
        senders,
        receivers,
        donors.T,
        norm_gain,
        corrupt_heads[0, 0],
        clean_heads[0, 0],
        out_weight[0],
        value_weight[0].T,
        residual[0, 0],
        clean_values[0, 0],
        queries[0, 0],
        key_vectors[0, 0],
    )
    return attended.reshape(1, 1, ROWS, -1)


def solution(mesh):
    return jax.shard_map(
        per_device,
        mesh=mesh,
        in_specs=(
            P("section", "ex", None, "tp"),
            P("section", "ex", None, "tp"),
            P("ex", None),
            P("section", "tp"),
            P("section", "tp", "ex"),
            P("section", "ex", None, "tp"),
            P("section", "tp"),
            P("section", "tp", "ex"),
            P("section", "ex", None, "tp"),
            P("section", "ex", None, "tp"),
            P("section", "ex", None, "tp"),
            P("section", "tp"),
        ),
        out_specs=P("section", "ex", None, "tp"),
        check_vma=False,
    )
```

```python
import math

import jax
import jax.numpy as jnp
from jax import lax
from jax.experimental import pallas as pl
from jax.experimental.pallas import tpu as pltpu
from jax.sharding import PartitionSpec as P

D = 8192
HD = 128
GROUP = 4
SEC = 4
EX = 16
TP = 4
ROWS = 512
HALF = 256
BF = jnp.bfloat16
F32 = jnp.float32
MESH = pl.DeviceIdType.MESH
CHIPS = EX // 2


def dot_nt(a, b):
    return lax.dot_general(a, b, (((1,), (1,)), ((), ())), preferred_element_type=F32)


def remote(src, dst, send, recv, device):
    return pltpu.make_async_remote_copy(
        src_ref=src,
        dst_ref=dst,
        send_sem=send,
        recv_sem=recv,
        device_id=device,
        device_id_type=MESH,
    )


def kernel(
    senders,
    receivers,
    donors,
    gain,
    corrupt_hbm,
    clean_hbm,
    weight_hbm,
    value_weight_hbm,
    residual_hbm,
    clean_values_hbm,
    queries_hbm,
    keys_hbm,
    out,
    arrived,
    patched,
    returned,
    weights,
    value_weights,
    differences,
    total,
    carried_out,
    carried_in,
    scaled,
    values_out,
    values_in,
    squares_out,
    squares_in,
    values,
    probabilities,
    residual,
    clean_values,
    queries,
    keys,
    corrupt_all,
    clean_all,
    weight_all,
    corrupt,
    clean,
    weight,
    flags,
    local_sem,
    patch_send,
    patch_recv,
    back_send,
    back_recv,
    piece_send,
    piece_recv,
    up_send,
    up_recv,
    down_send,
    down_recv,
    side_send,
    side_recv,
    diff_send,
    diff_recv,
    carry_send,
    carry_recv,
    value_send,
    value_recv,
    square_send,
    square_recv,
):
    sec = lax.axis_index("section")
    ex = lax.axis_index("ex")
    tp = lax.axis_index("tp")
    chip = ex // 2
    core = lax.rem(ex, 2)
    mine = TP * sec + tp
    group = SEC * tp + sec

    loads = [
        pltpu.make_async_copy(queries_hbm, queries, local_sem.at[0]),
        pltpu.make_async_copy(keys_hbm, keys, local_sem.at[1]),
        pltpu.make_async_copy(residual_hbm, residual, local_sem.at[2]),
        pltpu.make_async_copy(clean_values_hbm, clean_values, local_sem.at[3]),
        pltpu.make_async_copy(clean_hbm, clean_all, local_sem.at[4]),
    ]
    first_loads = [
        pltpu.make_async_copy(corrupt_hbm, corrupt_all, local_sem.at[5]),
        pltpu.make_async_copy(weight_hbm, weight_all, local_sem.at[6]),
        pltpu.make_async_copy(value_weight_hbm, value_weights.at[ex], local_sem.at[7]),
    ]
    for load in first_loads:
        load.start()

    barrier = pltpu.get_barrier_semaphore()

    @pl.loop(1, EX)
    def _(i):
        pl.semaphore_signal(
            barrier, inc=1, device_id={"ex": lax.rem(ex + i, EX)}, device_id_type=MESH
        )

    def plane_peer(i):
        other = lax.rem(mine + i, EX)
        return other // TP, lax.rem(other, TP)

    @pl.loop(1, EX)
    def _(i):
        s, t = plane_peer(i)
        pl.semaphore_signal(
            barrier, inc=1, device_id={"section": s, "tp": t}, device_id_type=MESH
        )

    heads_here = 2 * GROUP
    feature = lax.broadcasted_iota(jnp.int32, (heads_here * HD, HD), 0)
    lane = lax.broadcasted_iota(jnp.int32, (heads_here * HD, HD), 1)
    picks = []
    for i in (0, 1):
        head = senders[:, i : i + 1] - heads_here * tp
        picks.append((feature - lane == head * HD).astype(F32).astype(BF))
    pick = jnp.concatenate(picks, axis=1)
    first_loads[0].wait()
    corrupt[...] = (
        jnp.dot(corrupt_all[...], pick, preferred_element_type=F32)
        .astype(BF)
        .reshape(EX, ROWS // EX, 2 * HD)
    )

    pl.semaphore_wait(barrier, 2 * (EX - 1))

    @pl.loop(1, EX)
    def _(i):
        other = lax.rem(ex + i, EX)
        remote(
            corrupt.at[other], arrived.at[ex], patch_send.at[i], patch_recv.at[ex], {"ex": other}
        ).start()

    arrived[ex] = corrupt[ex]
    first_loads[1].wait()
    weight[...] = (
        lax.dot_general(
            weight_all[...], pick, (((0,), (0,)), ((), ())), preferred_element_type=F32
        )
        .astype(BF)
        .reshape(EX, ROWS // EX, 2 * HD)
    )

    @pl.loop(1, EX)
    def _(i):
        s, t = plane_peer(i)
        remote(
            weight.at[SEC * t + s],
            weights.at[ex, mine],
            piece_send.at[i],
            piece_recv.at[mine],
            {"section": s, "tp": t},
        ).start()

    weights[ex, mine] = weight[group]
    for load in loads:
        load.start()
    first_loads[2].wait()

    ring_up = 2 * lax.rem(chip + 1, CHIPS) + core
    ring_down = 2 * lax.rem(chip + CHIPS - 1, CHIPS) + core
    ring_side = 2 * chip + 1 - core

    def ring_copy(which, buffer, upward, origin, part, step):
        middle = buffer.shape[1] // 2
        ref = buffer.at[origin, pl.ds(part * middle, middle)]
        send, recv = (up_send, up_recv) if upward else (down_send, down_recv)
        index = 2 * step + part
        return remote(
            ref,
            ref,
            send.at[which, index],
            recv.at[which, index],
            {"ex": ring_up if upward else ring_down},
        )

    def to_side(which, buffer, origin, slot):
        ref = buffer.at[origin]
        remote(
            ref, ref, side_send.at[which, slot], side_recv.at[which, slot], {"ex": ring_side}
        ).start()

    def ring_start(which, buffer):
        for part in (0, 1):
            ring_copy(which, buffer, True, ex, part, 0).start()
            ring_copy(which, buffer, False, ex, part, 0).start()
        to_side(which, buffer, ex, 0)

    def ring_relay(which, buffer, step):
        above = 2 * lax.rem(chip + CHIPS - step, CHIPS) + core
        below = 2 * lax.rem(chip + step, CHIPS) + core
        for part in (0, 1):
            if step < 4 or part == 0:
                ring_copy(which, buffer, True, above, part, step - 1).wait_recv()
            if step < 3 or (step == 3 and part == 0):
                ring_copy(which, buffer, True, above, part, step).start()
            if step < 4 or part == 1:
                ring_copy(which, buffer, False, below, part, step - 1).wait_recv()
            if step < 3 or (step == 3 and part == 1):
                ring_copy(which, buffer, False, below, part, step).start()
        to_side(which, buffer, above, step)
        if step < 4:
            to_side(which, buffer, below, 4 + step)

    def ring_finish(which, buffer):
        side = 2 * chip + 1 - core
        for step in range(8):
            shift = CHIPS - step if step < 5 else step - 4
            block = buffer.at[2 * lax.rem(chip + shift, CHIPS) + 1 - core]
            remote(
                block, block, side_send.at[which, step], side_recv.at[which, step], {"ex": side}
            ).wait_recv()

    def ring_drain(which, buffer):
        for step in range(4):
            for part in (0, 1):
                if step < 3 or part == 0:
                    ring_copy(which, buffer, True, ex, part, step).wait_send()
                if step < 3 or part == 1:
                    ring_copy(which, buffer, False, ex, part, step).wait_send()
        block = buffer.at[ex]
        for slot in range(8):
            remote(
                block, block, side_send.at[which, slot], side_recv.at[which, slot], {"ex": ring_side}
            ).wait_send()

    def softmax(scores):
        exponent = jnp.exp(scores - jnp.max(scores, axis=-1, keepdims=True))
        return (exponent / jnp.sum(exponent, axis=-1, keepdims=True)).astype(BF)

    def weigh_heads(low, high):
        @pl.loop(low, high)
        def _(h):
            lanes = pl.ds(pl.multiple_of(h * HD, HD), HD)
            shared = pl.ds(pl.multiple_of(h // GROUP * HD, HD), HD)
            for half in (0, 1):
                length = HALF * (half + 1)
                scores = dot_nt(
                    queries[half * HALF : (half + 1) * HALF, lanes], keys[:length, shared]
                ) * (1.0 / math.sqrt(HD))
                row = lax.broadcasted_iota(jnp.int32, scores.shape, 0) + half * HALF
                column = lax.broadcasted_iota(jnp.int32, scores.shape, 1)
                scores = jnp.where(row >= column, scores, -jnp.inf)
                probabilities[h, half * HALF : (half + 1) * HALF, :length] = softmax(scores)

    block = ROWS // EX
    same = lax.broadcasted_iota(jnp.int32, (block, block), 0) == lax.broadcasted_iota(
        jnp.int32, (block, block), 1
    )
    donor = dot_nt(same.astype(F32).astype(BF), donors[...].astype(F32).astype(BF))
    row = lax.broadcasted_iota(jnp.int32, (block, ROWS), 0)
    column = lax.broadcasted_iota(jnp.int32, (block, ROWS), 1)
    offset = (column - row).astype(F32)
    onehot = jnp.concatenate(
        [
            (offset == donor[:, e : e + 1] * block).astype(F32).astype(BF)
            for e in range(EX)
        ],
        axis=0,
    )

    @pl.loop(1, EX)
    def _(i):
        other = lax.rem(ex + i, EX)
        remote(
            arrived.at[other], arrived.at[other], patch_send.at[i], patch_recv.at[other], {"ex": other}
        ).wait_recv()

    moved = jnp.dot(
        onehot, arrived[...].reshape(ROWS, 2 * HD), preferred_element_type=F32
    ).astype(BF)
    patched[...] = moved.reshape(EX, ROWS // EX, 2 * HD)

    @pl.loop(1, EX)
    def _(i):
        other = lax.rem(ex + i, EX)
        remote(
            patched.at[other], returned.at[ex], back_send.at[i], back_recv.at[ex], {"ex": other}
        ).start()

    returned[ex] = patched[ex]

    @pl.loop(1, EX)
    def _(i):
        other = lax.rem(mine + i, EX)
        remote(
            weights.at[ex, other],
            weights.at[ex, other],
            piece_send.at[i],
            piece_recv.at[other],
            {"ex": ex},
        ).wait_recv()

    ring_start(0, weights)
    loads[4].wait()
    clean[...] = jnp.dot(clean_all[...], pick, preferred_element_type=F32).astype(BF)
    for h in range(heads_here):
        flags[h : h + 1, :] = jnp.broadcast_to(receivers[:, h : h + 1], (1, HD))
    loads[0].wait()
    loads[1].wait()
    weigh_heads(0, 2)

    @pl.loop(1, EX)
    def _(i):
        other = lax.rem(ex + i, EX)
        remote(
            returned.at[other],
            returned.at[other],
            back_send.at[i],
            back_recv.at[other],
            {"ex": other},
        ).wait_recv()

    change = returned[...].reshape(ROWS, 2 * HD).astype(F32) - clean[...].astype(F32)
    differences[0, mine] = change[:HALF].astype(BF)
    differences[1, mine] = change[HALF:].astype(BF)

    axes = (("tp", "section"), ("section", "tp"))
    places = ((tp, sec), (sec, tp))

    def block_of(half, first, second):
        first, second = lax.rem(first + 8, 4), lax.rem(second + 8, 4)
        return TP * second + first if half == 0 else TP * first + second

    def difference_send(half, ref, block, axis, step, slot):
        here = sec if axis == "section" else tp
        remote(
            ref,
            ref,
            diff_send.at[half, slot],
            diff_recv.at[half, block],
            {axis: lax.rem(here + step + 4, 4)},
        ).start()

    def to_neighbours(half, phase, block, slot):
        ref = differences.at[half, block]
        difference_send(half, ref, block, axes[half][phase], 1, slot)
        difference_send(half, ref, block, axes[half][phase], -1, slot + 1)

    def pass_on(half, phase, block, step, slot):
        part = pl.ds(0, HALF // 2) if step > 0 else pl.ds(HALF // 2, HALF // 2)
        ref = differences.at[half, block, part]
        difference_send(half, ref, block, axes[half][phase], step, slot)

    def difference_wait(half, block):
        ref = differences.at[half, block]
        remote(ref, ref, diff_send.at[half, 0], diff_recv.at[half, block], {"ex": ex}).wait_recv()

    def second_phase(k):
        shift = (0, -1, 1, 2)[k]
        for half in (0, 1):
            first, second = places[half]
            for step in (1, -1):
                block = block_of(half, first + shift, second - step)
                difference_wait(half, block)
                pass_on(half, 1, block, step, 12 + 2 * k + (step < 0))

    for half in (0, 1):
        to_neighbours(half, 0, mine, 0)
    for half in (0, 1):
        to_neighbours(half, 1, mine, 2)
    for half in (0, 1):
        first, second = places[half]
        for step in (1, -1):
            block = block_of(half, first - step, second)
            difference_wait(half, block)
            pass_on(half, 0, block, step, 10 + (step < 0))
            to_neighbours(half, 1, block, 4 if step > 0 else 6)
    ring_relay(0, weights, 1)
    second_phase(0)
    ring_relay(0, weights, 2)
    for half in (0, 1):
        first, second = places[half]
        block = block_of(half, first + 2, second)
        difference_wait(half, block)
        to_neighbours(half, 1, block, 8)
    second_phase(1)
    ring_relay(0, weights, 3)
    second_phase(2)
    ring_relay(0, weights, 4)
    ring_start(1, value_weights)
    second_phase(3)
    ring_finish(0, weights)

    def carry(half):
        @pl.loop(0, SEC)
        def _(r):
            for t in range(TP):
                block = TP * r + t
                opposite = lax.rem(sec + 2, SEC) if half == 0 else lax.rem(tp + 2, TP)

                @pl.when((r if half == 0 else t) == opposite)
                def _():
                    difference_wait(half, block)

            term = dot_nt(differences[half, TP * r], weights[:, TP * r].reshape(ROWS, 2 * HD))
            for t in range(1, TP):
                term += dot_nt(
                    differences[half, TP * r + t], weights[:, TP * r + t].reshape(ROWS, 2 * HD)
                )

            @pl.when(r == 0)
            def _():
                total[...] = term

            @pl.when(r > 0)
            def _():
                total[...] += term

            rounded = total[...].astype(BF)
            for t in range(TP):
                carried_out[half, r, t] = rounded[:, t * HD : (t + 1) * HD]
                here = jnp.logical_and(r == sec, t == tp)

                @pl.when(here)
                def _():
                    carried_in[half, group] = carried_out[half, r, t]

                @pl.when(jnp.logical_not(here))
                def _():
                    remote(
                        carried_out.at[half, r, t],
                        carried_in.at[half, group],
                        carry_send.at[half, TP * r + t],
                        carry_recv.at[half, group],
                        {"section": r, "tp": t},
                    ).start()

    carry(0)
    ring_relay(1, value_weights, 1)
    carry(1)
    ring_relay(1, value_weights, 2)
    weigh_heads(2, 5)
    ring_relay(1, value_weights, 3)
    weigh_heads(5, 8)
    ring_relay(1, value_weights, 4)
    ring_finish(1, value_weights)
    loads[2].wait()
    loads[3].wait()

    source = lax.broadcasted_iota(jnp.int32, (ROWS, ROWS), 0)
    column = lax.broadcasted_iota(jnp.int32, (ROWS, ROWS), 1)
    place = source // 32 % 4 * 128 + source // 128 * 32 + source % 32
    order = (place == column).astype(F32).astype(BF)

    def finish_stream(half):
        rows = slice(half * HALF, (half + 1) * HALF)

        @pl.loop(1, EX)
        def _(i):
            other = lax.rem(group + i, EX)
            remote(
                carried_in.at[half, other],
                carried_in.at[half, other],
                carry_send.at[half, 0],
                carry_recv.at[half, other],
                {"ex": ex},
            ).wait_recv()

        square = jnp.zeros((HALF, HD), F32)
        for g in range(4):
            pieces = jnp.concatenate([carried_in[half, 4 * g + q] for q in range(4)], axis=1)
            ordered = jnp.dot(pieces, order, preferred_element_type=F32)
            for j in range(4):
                lanes = slice(j * ROWS + g * HD, j * ROWS + (g + 1) * HD)
                stream = residual[rows, lanes].astype(F32) + ordered[:, j * HD : (j + 1) * HD]
                square += stream * stream
                scaled[rows, lanes] = (stream * gain[:, lanes].astype(F32)).astype(BF)
        sums = jnp.broadcast_to(jnp.sum(square, axis=1, keepdims=True), (HALF, HD))
        squares_out[half] = jnp.transpose(sums)[:8]
        squares_in[half, tp] = squares_out[half]
        for i in range(1, TP):
            other = lax.rem(tp + i, TP)
            remote(
                squares_out.at[half],
                squares_in.at[half, tp],
                square_send.at[half, i],
                square_recv.at[half, tp],
                {"tp": other},
            ).start()

        @pl.loop(1, TP + 1)
        def _(i):
            other = lax.rem(tp + i, TP)
            columns = value_weights[pl.ds(4 * other, 4)].reshape(2 * HD, SEC * ROWS)
            values_out[half, other] = dot_nt(scaled[rows, :], columns).astype(BF)

            @pl.when(i < TP)
            def _():
                remote(
                    values_out.at[half, other],
                    values_in.at[half, tp],
                    value_send.at[half, other],
                    value_recv.at[half, tp],
                    {"tp": other},
                ).start()

        values_in[half, tp] = values_out[half, tp]

    def attend(half):
        rows = slice(half * HALF, (half + 1) * HALF)
        for i in range(1, TP):
            other = lax.rem(tp + i, TP)
            remote(
                values_in.at[half, other],
                values_in.at[half, other],
                value_send.at[half, 0],
                value_recv.at[half, other],
                {"ex": ex},
            ).wait_recv()
            remote(
                squares_in.at[half, other],
                squares_in.at[half, other],
                square_send.at[half, 0],
                square_recv.at[half, other],
                {"ex": ex},
            ).wait_recv()
        squares = (squares_in[half, 0] + squares_in[half, 1]) + (
            squares_in[half, 2] + squares_in[half, 3]
        )
        scale = lax.rsqrt(squares / D + 1e-05)
        scale = jnp.transpose(jnp.concatenate([scale] * 16, axis=0))
        for g in (0, 1):
            lanes = slice(g * HD, (g + 1) * HD)
            summed = values_in[half, 0, :, lanes].astype(F32)
            for t in range(1, TP):
                summed += values_in[half, t, :, lanes].astype(F32)
            values[rows, lanes] = (summed * scale).astype(BF)
        length = HALF * (half + 1)

        @pl.loop(0, 2 * GROUP)
        def _(h):
            shared = pl.ds(pl.multiple_of(h // GROUP * HD, HD), HD)
            flag = jnp.broadcast_to(flags[pl.ds(h, 1), :], (length, HD)) == 1
            chosen = jnp.where(
                flag,
                values[:length, shared].astype(F32),
                clean_values[:length, shared].astype(F32),
            ).astype(BF)
            out[rows, pl.ds(pl.multiple_of(h * HD, HD), HD)] = jnp.dot(
                probabilities[h, rows, :length], chosen, preferred_element_type=F32
            ).astype(BF)

    finish_stream(0)
    finish_stream(1)
    attend(0)
    attend(1)

    @pl.loop(1, EX)
    def _(i):
        remote(corrupt.at[0], arrived.at[0], patch_send.at[i], patch_recv.at[0], {"ex": 0}).wait_send()
        remote(patched.at[0], returned.at[0], back_send.at[i], back_recv.at[0], {"ex": 0}).wait_send()
        remote(
            weight.at[0], weights.at[0, 0], piece_send.at[i], piece_recv.at[0], {"ex": 0}
        ).wait_send()

    ring_drain(0, weights)
    ring_drain(1, value_weights)
    for half in (0, 1):

        @pl.loop(0, 10)
        def _(i):
            ref = differences.at[half, 0]
            remote(ref, ref, diff_send.at[half, i], diff_recv.at[half, 0], {"ex": 0}).wait_send()
            ref = differences.at[half, 0, pl.ds(0, HALF // 2)]
            remote(
                ref, ref, diff_send.at[half, 10 + i], diff_recv.at[half, 0], {"ex": 0}
            ).wait_send()

        @pl.loop(1, EX)
        def _(i):
            other = lax.rem(mine + i, EX)
            remote(
                carried_out.at[half, 0, 0],
                carried_in.at[half, 0],
                carry_send.at[half, other],
                carry_recv.at[half, 0],
                {"ex": 0},
            ).wait_send()

        for i in range(1, TP):
            other = lax.rem(tp + i, TP)
            remote(
                values_out.at[half, 0],
                values_in.at[half, 0],
                value_send.at[half, other],
                value_recv.at[half, 0],
                {"ex": 0},
            ).wait_send()
            remote(
                squares_out.at[half],
                squares_in.at[half, 0],
                square_send.at[half, i],
                square_recv.at[half, 0],
                {"ex": 0},
            ).wait_send()


def per_device(
    clean_heads,
    corrupt_heads,
    donors,
    senders,
    out_weight,
    residual,
    norm_gain,
    value_weight,
    clean_values,
    queries,
    key_vectors,
    receivers,
):
    dma = pltpu.SemaphoreType.DMA
    vmem = pl.BlockSpec(memory_space=pltpu.VMEM)
    hbm = pl.BlockSpec(memory_space=pl.ANY)
    attended = pl.pallas_call(
        kernel,
        out_shape=jax.ShapeDtypeStruct((ROWS, 2 * GROUP * HD), BF),
        in_specs=[vmem] * 4 + [hbm] * 8,
        out_specs=vmem,
        scratch_shapes=[
            pltpu.VMEM((EX, 32, 2 * HD), BF),
            pltpu.VMEM((EX, 32, 2 * HD), BF),
            pltpu.VMEM((EX, 32, 2 * HD), BF),
            pltpu.VMEM((EX, EX, 32, 2 * HD), BF),
            pltpu.VMEM((EX, 64, SEC * ROWS), BF),
            pltpu.VMEM((2, EX, HALF, 2 * HD), BF),
            pltpu.VMEM((HALF, ROWS), F32),
            pltpu.VMEM((2, SEC, TP, HALF, HD), BF),
            pltpu.VMEM((2, EX, HALF, HD), BF),
            pltpu.VMEM((ROWS, SEC * ROWS), BF),
            pltpu.VMEM((2, TP, HALF, 2 * HD), BF),
            pltpu.VMEM((2, TP, HALF, 2 * HD), BF),
            pltpu.VMEM((2, 8, HALF), F32),
            pltpu.VMEM((2, TP, 8, HALF), F32),
            pltpu.VMEM((ROWS, 2 * HD), BF),
            pltpu.VMEM((2 * GROUP, ROWS, ROWS), BF),
            pltpu.VMEM((ROWS, SEC * ROWS), BF),
            pltpu.VMEM((ROWS, 2 * HD), BF),
            pltpu.VMEM((ROWS, 2 * GROUP * HD), BF),
            pltpu.VMEM((ROWS, 2 * HD), BF),
            pltpu.VMEM((ROWS, 8 * HD), BF),
            pltpu.VMEM((ROWS, 8 * HD), BF),
            pltpu.VMEM((8 * HD, ROWS), BF),
            pltpu.VMEM((EX, 32, 2 * HD), BF),
            pltpu.VMEM((ROWS, 2 * HD), BF),
            pltpu.VMEM((EX, 32, 2 * HD), BF),
            pltpu.VMEM((2 * GROUP, HD), jnp.int32),
            dma((8,)),
            dma((EX,)),
            dma((EX,)),
            dma((EX,)),
            dma((EX,)),
            dma((EX,)),
            dma((EX,)),
            dma((2, 8)),
            dma((2, 8)),
            dma((2, 8)),
            dma((2, 8)),
            dma((2, 8)),
            dma((2, 8)),
            dma((2, 20)),
            dma((2, EX)),
            dma((2, EX)),
            dma((2, EX)),
            dma((2, TP)),
            dma((2, TP)),
            dma((2, TP)),
            dma((2, TP)),
        ],
        compiler_params=pltpu.CompilerParams(
            collective_id=0, has_side_effects=True, vmem_limit_bytes=56 * 2**20
        ),
    )(
        senders,
        receivers,
        donors.T,
        norm_gain,
        corrupt_heads[0, 0],
        clean_heads[0, 0],
        out_weight[0],
        value_weight[0].T,
        residual[0, 0],
        clean_values[0, 0],
        queries[0, 0],
        key_vectors[0, 0],
    )
    return attended.reshape(1, 1, ROWS, -1)


def solution(mesh):
    return jax.shard_map(
        per_device,
        mesh=mesh,
        in_specs=(
            P("section", "ex", None, "tp"),
            P("section", "ex", None, "tp"),
            P("ex", None),
            P("section", "tp"),
            P("section", "tp", "ex"),
            P("section", "ex", None, "tp"),
            P("section", "tp"),
            P("section", "tp", "ex"),
            P("section", "ex", None, "tp"),
            P("section", "ex", None, "tp"),
            P("section", "ex", None, "tp"),
            P("section", "tp"),
        ),
        out_specs=P("section", "ex", None, "tp"),
        check_vma=False,
    )
```

```python
import math

import jax
import jax.numpy as jnp
from jax import lax
from jax.experimental import pallas as pl
from jax.experimental.pallas import tpu as pltpu
from jax.sharding import PartitionSpec as P

D = 8192
HD = 128
GROUP = 4
SEC = 4
EX = 16
TP = 4
ROWS = 512
HALF = 256
BF = jnp.bfloat16
F32 = jnp.float32
MESH = pl.DeviceIdType.MESH
CHIPS = EX // 2


def dot_nt(a, b):
    return lax.dot_general(a, b, (((1,), (1,)), ((), ())), preferred_element_type=F32)


def remote(src, dst, send, recv, device):
    return pltpu.make_async_remote_copy(
        src_ref=src,
        dst_ref=dst,
        send_sem=send,
        recv_sem=recv,
        device_id=device,
        device_id_type=MESH,
    )


def kernel(
    senders,
    receivers,
    donors,
    gain,
    corrupt_hbm,
    clean_hbm,
    weight_hbm,
    value_weight_hbm,
    residual_hbm,
    clean_values_hbm,
    queries_hbm,
    keys_hbm,
    out,
    arrived,
    patched,
    returned,
    weights,
    value_weights,
    differences,
    total,
    carried_out,
    carried_in,
    scaled,
    values_out,
    values_in,
    squares_out,
    squares_in,
    values,
    probabilities,
    residual,
    clean_values,
    queries,
    keys,
    corrupt_all,
    clean_all,
    weight_all,
    corrupt,
    clean,
    weight,
    flags,
    local_sem,
    patch_send,
    patch_recv,
    back_send,
    back_recv,
    piece_send,
    piece_recv,
    up_send,
    up_recv,
    down_send,
    down_recv,
    side_send,
    side_recv,
    diff_send,
    diff_recv,
    carry_send,
    carry_recv,
    value_send,
    value_recv,
    square_send,
    square_recv,
):
    sec = lax.axis_index("section")
    ex = lax.axis_index("ex")
    tp = lax.axis_index("tp")
    chip = ex // 2
    core = lax.rem(ex, 2)
    mine = TP * sec + tp
    group = SEC * tp + sec

    loads = [
        pltpu.make_async_copy(queries_hbm, queries, local_sem.at[0]),
        pltpu.make_async_copy(keys_hbm, keys, local_sem.at[1]),
        pltpu.make_async_copy(residual_hbm, residual, local_sem.at[2]),
        pltpu.make_async_copy(clean_values_hbm, clean_values, local_sem.at[3]),
        pltpu.make_async_copy(clean_hbm, clean_all, local_sem.at[4]),
    ]
    first_loads = [
        pltpu.make_async_copy(corrupt_hbm, corrupt_all, local_sem.at[5]),
        pltpu.make_async_copy(weight_hbm, weight_all, local_sem.at[6]),
        pltpu.make_async_copy(value_weight_hbm, value_weights.at[ex], local_sem.at[7]),
    ]
    for load in first_loads:
        load.start()

    barrier = pltpu.get_barrier_semaphore()

    @pl.loop(1, EX)
    def _(i):
        pl.semaphore_signal(
            barrier, inc=1, device_id={"ex": lax.rem(ex + i, EX)}, device_id_type=MESH
        )

    def plane_peer(i):
        other = lax.rem(mine + i, EX)
        return other // TP, lax.rem(other, TP)

    @pl.loop(1, EX)
    def _(i):
        s, t = plane_peer(i)
        pl.semaphore_signal(
            barrier, inc=1, device_id={"section": s, "tp": t}, device_id_type=MESH
        )

    heads_here = 2 * GROUP
    feature = lax.broadcasted_iota(jnp.int32, (heads_here * HD, HD), 0)
    lane = lax.broadcasted_iota(jnp.int32, (heads_here * HD, HD), 1)
    picks = []
    for i in (0, 1):
        head = senders[:, i : i + 1] - heads_here * tp
        picks.append((feature - lane == head * HD).astype(F32).astype(BF))
    pick = jnp.concatenate(picks, axis=1)
    first_loads[0].wait()
    corrupt[...] = (
        jnp.dot(corrupt_all[...], pick, preferred_element_type=F32)
        .astype(BF)
        .reshape(EX, ROWS // EX, 2 * HD)
    )

    pl.semaphore_wait(barrier, 2 * (EX - 1))

    @pl.loop(1, EX)
    def _(i):
        other = lax.rem(ex + i, EX)
        remote(
            corrupt.at[other], arrived.at[ex], patch_send.at[i], patch_recv.at[ex], {"ex": other}
        ).start()

    arrived[ex] = corrupt[ex]
    first_loads[1].wait()
    weight[...] = (
        lax.dot_general(
            weight_all[...], pick, (((0,), (0,)), ((), ())), preferred_element_type=F32
        )
        .astype(BF)
        .reshape(EX, ROWS // EX, 2 * HD)
    )

    @pl.loop(1, EX)
    def _(i):
        s, t = plane_peer(i)
        remote(
            weight.at[SEC * t + s],
            weights.at[ex, mine],
            piece_send.at[i],
            piece_recv.at[mine],
            {"section": s, "tp": t},
        ).start()

    weights[ex, mine] = weight[group]
    for load in loads:
        load.start()
    first_loads[2].wait()

    ring_up = 2 * lax.rem(chip + 1, CHIPS) + core
    ring_down = 2 * lax.rem(chip + CHIPS - 1, CHIPS) + core
    ring_side = 2 * chip + 1 - core

    def ring_copy(which, buffer, upward, origin, part, step):
        middle = buffer.shape[1] // 2
        ref = buffer.at[origin, pl.ds(part * middle, middle)]
        send, recv = (up_send, up_recv) if upward else (down_send, down_recv)
        index = 2 * step + part
        return remote(
            ref,
            ref,
            send.at[which, index],
            recv.at[which, index],
            {"ex": ring_up if upward else ring_down},
        )

    def to_side(which, buffer, origin, slot):
        ref = buffer.at[origin]
        remote(
            ref, ref, side_send.at[which, slot], side_recv.at[which, slot], {"ex": ring_side}
        ).start()

    def ring_start(which, buffer):
        for part in (0, 1):
            ring_copy(which, buffer, True, ex, part, 0).start()
            ring_copy(which, buffer, False, ex, part, 0).start()
        to_side(which, buffer, ex, 0)

    def ring_relay(which, buffer, step):
        above = 2 * lax.rem(chip + CHIPS - step, CHIPS) + core
        below = 2 * lax.rem(chip + step, CHIPS) + core
        for part in (0, 1):
            if step < 4 or part == 0:
                ring_copy(which, buffer, True, above, part, step - 1).wait_recv()
            if step < 3 or (step == 3 and part == 0):
                ring_copy(which, buffer, True, above, part, step).start()
            if step < 4 or part == 1:
                ring_copy(which, buffer, False, below, part, step - 1).wait_recv()
            if step < 3 or (step == 3 and part == 1):
                ring_copy(which, buffer, False, below, part, step).start()
        to_side(which, buffer, above, step)
        if step < 4:
            to_side(which, buffer, below, 4 + step)

    def ring_finish(which, buffer):
        side = 2 * chip + 1 - core
        for step in range(8):
            shift = CHIPS - step if step < 5 else step - 4
            block = buffer.at[2 * lax.rem(chip + shift, CHIPS) + 1 - core]
            remote(
                block, block, side_send.at[which, step], side_recv.at[which, step], {"ex": side}
            ).wait_recv()

    def ring_drain(which, buffer):
        for step in range(4):
            for part in (0, 1):
                if step < 3 or part == 0:
                    ring_copy(which, buffer, True, ex, part, step).wait_send()
                if step < 3 or part == 1:
                    ring_copy(which, buffer, False, ex, part, step).wait_send()
        block = buffer.at[ex]
        for slot in range(8):
            remote(
                block, block, side_send.at[which, slot], side_recv.at[which, slot], {"ex": ring_side}
            ).wait_send()

    def softmax(scores):
        exponent = jnp.exp(scores - jnp.max(scores, axis=-1, keepdims=True))
        return (exponent / jnp.sum(exponent, axis=-1, keepdims=True)).astype(BF)

    def weigh_heads(low, high):
        @pl.loop(low, high)
        def _(h):
            lanes = pl.ds(pl.multiple_of(h * HD, HD), HD)
            shared = pl.ds(pl.multiple_of(h // GROUP * HD, HD), HD)
            for half in (0, 1):
                length = HALF * (half + 1)
                scores = dot_nt(
                    queries[half * HALF : (half + 1) * HALF, lanes], keys[:length, shared]
                ) * (1.0 / math.sqrt(HD))
                row = lax.broadcasted_iota(jnp.int32, scores.shape, 0) + half * HALF
                column = lax.broadcasted_iota(jnp.int32, scores.shape, 1)
                scores = jnp.where(row >= column, scores, -jnp.inf)
                probabilities[h, half * HALF : (half + 1) * HALF, :length] = softmax(scores)

    block = ROWS // EX
    same = lax.broadcasted_iota(jnp.int32, (block, block), 0) == lax.broadcasted_iota(
        jnp.int32, (block, block), 1
    )
    donor = dot_nt(same.astype(F32).astype(BF), donors[...].astype(F32).astype(BF))
    row = lax.broadcasted_iota(jnp.int32, (block, ROWS), 0)
    column = lax.broadcasted_iota(jnp.int32, (block, ROWS), 1)
    offset = (column - row).astype(F32)
    onehot = jnp.concatenate(
        [
            (offset == donor[:, e : e + 1] * block).astype(F32).astype(BF)
            for e in range(EX)
        ],
        axis=0,
    )

    @pl.loop(1, EX)
    def _(i):
        other = lax.rem(ex + i, EX)
        remote(
            arrived.at[other], arrived.at[other], patch_send.at[i], patch_recv.at[other], {"ex": other}
        ).wait_recv()

    moved = jnp.dot(
        onehot, arrived[...].reshape(ROWS, 2 * HD), preferred_element_type=F32
    ).astype(BF)
    patched[...] = moved.reshape(EX, ROWS // EX, 2 * HD)

    @pl.loop(1, EX)
    def _(i):
        other = lax.rem(ex + i, EX)
        remote(
            patched.at[other], returned.at[ex], back_send.at[i], back_recv.at[ex], {"ex": other}
        ).start()

    returned[ex] = patched[ex]

    @pl.loop(1, EX)
    def _(i):
        other = lax.rem(mine + i, EX)
        remote(
            weights.at[ex, other],
            weights.at[ex, other],
            piece_send.at[i],
            piece_recv.at[other],
            {"ex": ex},
        ).wait_recv()

    ring_start(0, weights)
    loads[4].wait()
    clean[...] = jnp.dot(clean_all[...], pick, preferred_element_type=F32).astype(BF)
    for h in range(heads_here):
        flags[h : h + 1, :] = jnp.broadcast_to(receivers[:, h : h + 1], (1, HD))
    loads[0].wait()
    loads[1].wait()
    weigh_heads(0, 2)

    @pl.loop(1, EX)
    def _(i):
        other = lax.rem(ex + i, EX)
        remote(
            returned.at[other],
            returned.at[other],
            back_send.at[i],
            back_recv.at[other],
            {"ex": other},
        ).wait_recv()

    change = returned[...].reshape(ROWS, 2 * HD).astype(F32) - clean[...].astype(F32)
    differences[0, mine] = change[:HALF].astype(BF)
    differences[1, mine] = change[HALF:].astype(BF)

    axes = (("tp", "section"), ("section", "tp"))
    places = ((tp, sec), (sec, tp))

    def block_of(half, first, second):
        first, second = lax.rem(first + 8, 4), lax.rem(second + 8, 4)
        return TP * second + first if half == 0 else TP * first + second

    def difference_send(half, ref, block, axis, step, slot):
        here = sec if axis == "section" else tp
        remote(
            ref,
            ref,
            diff_send.at[half, slot],
            diff_recv.at[half, block],
            {axis: lax.rem(here + step + 4, 4)},
        ).start()

    def to_neighbours(half, phase, block, slot):
        ref = differences.at[half, block]
        difference_send(half, ref, block, axes[half][phase], 1, slot)
        difference_send(half, ref, block, axes[half][phase], -1, slot + 1)

    def pass_on(half, phase, block, step, slot):
        part = pl.ds(0, HALF // 2) if step > 0 else pl.ds(HALF // 2, HALF // 2)
        ref = differences.at[half, block, part]
        difference_send(half, ref, block, axes[half][phase], step, slot)

    def difference_wait(half, block):
        ref = differences.at[half, block]
        remote(ref, ref, diff_send.at[half, 0], diff_recv.at[half, block], {"ex": ex}).wait_recv()

    def second_phase(k):
        shift = (0, -1, 1, 2)[k]
        for half in (0, 1):
            first, second = places[half]
            for step in (1, -1):
                block = block_of(half, first + shift, second - step)
                difference_wait(half, block)
                pass_on(half, 1, block, step, 12 + 2 * k + (step < 0))

    for half in (0, 1):
        to_neighbours(half, 0, mine, 0)
    for half in (0, 1):
        to_neighbours(half, 1, mine, 2)
    for half in (0, 1):
        first, second = places[half]
        for step in (1, -1):
            block = block_of(half, first - step, second)
            difference_wait(half, block)
            pass_on(half, 0, block, step, 10 + (step < 0))
            to_neighbours(half, 1, block, 4 if step > 0 else 6)
    ring_relay(0, weights, 1)
    second_phase(0)
    ring_relay(0, weights, 2)
    for half in (0, 1):
        first, second = places[half]
        block = block_of(half, first + 2, second)
        difference_wait(half, block)
        to_neighbours(half, 1, block, 8)
    second_phase(1)
    second_phase(2)
    ring_relay(0, weights, 3)
    second_phase(3)
    ring_relay(0, weights, 4)
    ring_start(1, value_weights)
    ring_finish(0, weights)

    def carry(half):
        @pl.loop(0, SEC)
        def _(r):
            for t in range(TP):
                block = TP * r + t
                opposite = lax.rem(sec + 2, SEC) if half == 0 else lax.rem(tp + 2, TP)

                @pl.when((r if half == 0 else t) == opposite)
                def _():
                    difference_wait(half, block)

            term = dot_nt(differences[half, TP * r], weights[:, TP * r].reshape(ROWS, 2 * HD))
            for t in range(1, TP):
                term += dot_nt(
                    differences[half, TP * r + t], weights[:, TP * r + t].reshape(ROWS, 2 * HD)
                )

            @pl.when(r == 0)
            def _():
                total[...] = term

            @pl.when(r > 0)
            def _():
                total[...] += term

            rounded = total[...].astype(BF)
            for t in range(TP):
                carried_out[half, r, t] = rounded[:, t * HD : (t + 1) * HD]
                here = jnp.logical_and(r == sec, t == tp)

                @pl.when(here)
                def _():
                    carried_in[half, group] = carried_out[half, r, t]

                @pl.when(jnp.logical_not(here))
                def _():
                    remote(
                        carried_out.at[half, r, t],
                        carried_in.at[half, group],
                        carry_send.at[half, TP * r + t],
                        carry_recv.at[half, group],
                        {"section": r, "tp": t},
                    ).start()

    carry(0)
    ring_relay(1, value_weights, 1)
    carry(1)
    ring_relay(1, value_weights, 2)
    weigh_heads(2, 4)
    ring_relay(1, value_weights, 3)
    weigh_heads(4, 6)
    ring_relay(1, value_weights, 4)
    @pl.loop(1, EX)
    def _(i):
        remote(corrupt.at[0], arrived.at[0], patch_send.at[i], patch_recv.at[0], {"ex": 0}).wait_send()
        remote(patched.at[0], returned.at[0], back_send.at[i], back_recv.at[0], {"ex": 0}).wait_send()
        remote(
            weight.at[0], weights.at[0, 0], piece_send.at[i], piece_recv.at[0], {"ex": 0}
        ).wait_send()

    ring_drain(0, weights)
    for half in (0, 1):

        @pl.loop(0, 10)
        def _(i):
            ref = differences.at[half, 0]
            remote(ref, ref, diff_send.at[half, i], diff_recv.at[half, 0], {"ex": 0}).wait_send()
            ref = differences.at[half, 0, pl.ds(0, HALF // 2)]
            remote(
                ref, ref, diff_send.at[half, 10 + i], diff_recv.at[half, 0], {"ex": 0}
            ).wait_send()

    weigh_heads(6, 8)
    ring_finish(1, value_weights)
    loads[2].wait()
    loads[3].wait()

    source = lax.broadcasted_iota(jnp.int32, (ROWS, ROWS), 0)
    column = lax.broadcasted_iota(jnp.int32, (ROWS, ROWS), 1)
    place = source // 32 % 4 * 128 + source // 128 * 32 + source % 32
    order = (place == column).astype(F32).astype(BF)

    def finish_stream(half):
        rows = slice(half * HALF, (half + 1) * HALF)

        @pl.loop(1, EX)
        def _(i):
            other = lax.rem(group + i, EX)
            remote(
                carried_in.at[half, other],
                carried_in.at[half, other],
                carry_send.at[half, 0],
                carry_recv.at[half, other],
                {"ex": ex},
            ).wait_recv()

        square = jnp.zeros((HALF, HD), F32)
        for g in range(4):
            pieces = jnp.concatenate([carried_in[half, 4 * g + q] for q in range(4)], axis=1)
            ordered = jnp.dot(pieces, order, preferred_element_type=F32)
            for j in range(4):
                lanes = slice(j * ROWS + g * HD, j * ROWS + (g + 1) * HD)
                stream = residual[rows, lanes].astype(F32) + ordered[:, j * HD : (j + 1) * HD]
                square += stream * stream
                scaled[rows, lanes] = (stream * gain[:, lanes].astype(F32)).astype(BF)
        sums = jnp.broadcast_to(jnp.sum(square, axis=1, keepdims=True), (HALF, HD))
        squares_out[half] = jnp.transpose(sums)[:8]
        squares_in[half, tp] = squares_out[half]
        for i in range(1, TP):
            other = lax.rem(tp + i, TP)
            remote(
                squares_out.at[half],
                squares_in.at[half, tp],
                square_send.at[half, i],
                square_recv.at[half, tp],
                {"tp": other},
            ).start()

        @pl.loop(1, TP + 1)
        def _(i):
            other = lax.rem(tp + i, TP)
            columns = value_weights[pl.ds(4 * other, 4)].reshape(2 * HD, SEC * ROWS)
            values_out[half, other] = dot_nt(scaled[rows, :], columns).astype(BF)

            @pl.when(i < TP)
            def _():
                remote(
                    values_out.at[half, other],
                    values_in.at[half, tp],
                    value_send.at[half, other],
                    value_recv.at[half, tp],
                    {"tp": other},
                ).start()

        values_in[half, tp] = values_out[half, tp]

    def attend(half):
        rows = slice(half * HALF, (half + 1) * HALF)
        for i in range(1, TP):
            other = lax.rem(tp + i, TP)
            remote(
                values_in.at[half, other],
                values_in.at[half, other],
                value_send.at[half, 0],
                value_recv.at[half, other],
                {"ex": ex},
            ).wait_recv()
            remote(
                squares_in.at[half, other],
                squares_in.at[half, other],
                square_send.at[half, 0],
                square_recv.at[half, other],
                {"ex": ex},
            ).wait_recv()
        squares = (squares_in[half, 0] + squares_in[half, 1]) + (
            squares_in[half, 2] + squares_in[half, 3]
        )
        scale = lax.rsqrt(squares / D + 1e-05)
        scale = jnp.transpose(jnp.concatenate([scale] * 16, axis=0))
        for g in (0, 1):
            lanes = slice(g * HD, (g + 1) * HD)
            summed = values_in[half, 0, :, lanes].astype(F32)
            for t in range(1, TP):
                summed += values_in[half, t, :, lanes].astype(F32)
            values[rows, lanes] = (summed * scale).astype(BF)
        length = HALF * (half + 1)

        @pl.loop(0, 2 * GROUP)
        def _(h):
            shared = pl.ds(pl.multiple_of(h // GROUP * HD, HD), HD)
            flag = jnp.broadcast_to(flags[pl.ds(h, 1), :], (length, HD)) == 1
            chosen = jnp.where(
                flag,
                values[:length, shared].astype(F32),
                clean_values[:length, shared].astype(F32),
            ).astype(BF)
            out[rows, pl.ds(pl.multiple_of(h * HD, HD), HD)] = jnp.dot(
                probabilities[h, rows, :length], chosen, preferred_element_type=F32
            ).astype(BF)

    finish_stream(0)
    finish_stream(1)
    ring_drain(1, value_weights)
    for half in (0, 1):

        @pl.loop(1, EX)
        def _(i):
            other = lax.rem(mine + i, EX)
            remote(
                carried_out.at[half, 0, 0],
                carried_in.at[half, 0],
                carry_send.at[half, other],
                carry_recv.at[half, 0],
                {"ex": 0},
            ).wait_send()

    attend(0)
    attend(1)

    for half in (0, 1):
        for i in range(1, TP):
            other = lax.rem(tp + i, TP)
            remote(
                values_out.at[half, 0],
                values_in.at[half, 0],
                value_send.at[half, other],
                value_recv.at[half, 0],
                {"ex": 0},
            ).wait_send()
            remote(
                squares_out.at[half],
                squares_in.at[half, 0],
                square_send.at[half, i],
                square_recv.at[half, 0],
                {"ex": 0},
            ).wait_send()


def per_device(
    clean_heads,
    corrupt_heads,
    donors,
    senders,
    out_weight,
    residual,
    norm_gain,
    value_weight,
    clean_values,
    queries,
    key_vectors,
    receivers,
):
    dma = pltpu.SemaphoreType.DMA
    vmem = pl.BlockSpec(memory_space=pltpu.VMEM)
    hbm = pl.BlockSpec(memory_space=pl.ANY)
    attended = pl.pallas_call(
        kernel,
        out_shape=jax.ShapeDtypeStruct((ROWS, 2 * GROUP * HD), BF),
        in_specs=[vmem] * 4 + [hbm] * 8,
        out_specs=vmem,
        scratch_shapes=[
            pltpu.VMEM((EX, 32, 2 * HD), BF),
            pltpu.VMEM((EX, 32, 2 * HD), BF),
            pltpu.VMEM((EX, 32, 2 * HD), BF),
            pltpu.VMEM((EX, EX, 32, 2 * HD), BF),
            pltpu.VMEM((EX, 64, SEC * ROWS), BF),
            pltpu.VMEM((2, EX, HALF, 2 * HD), BF),
            pltpu.VMEM((HALF, ROWS), F32),
            pltpu.VMEM((2, SEC, TP, HALF, HD), BF),
            pltpu.VMEM((2, EX, HALF, HD), BF),
            pltpu.VMEM((ROWS, SEC * ROWS), BF),
            pltpu.VMEM((2, TP, HALF, 2 * HD), BF),
            pltpu.VMEM((2, TP, HALF, 2 * HD), BF),
            pltpu.VMEM((2, 8, HALF), F32),
            pltpu.VMEM((2, TP, 8, HALF), F32),
            pltpu.VMEM((ROWS, 2 * HD), BF),
            pltpu.VMEM((2 * GROUP, ROWS, ROWS), BF),
            pltpu.VMEM((ROWS, SEC * ROWS), BF),
            pltpu.VMEM((ROWS, 2 * HD), BF),
            pltpu.VMEM((ROWS, 2 * GROUP * HD), BF),
            pltpu.VMEM((ROWS, 2 * HD), BF),
            pltpu.VMEM((ROWS, 8 * HD), BF),
            pltpu.VMEM((ROWS, 8 * HD), BF),
            pltpu.VMEM((8 * HD, ROWS), BF),
            pltpu.VMEM((EX, 32, 2 * HD), BF),
            pltpu.VMEM((ROWS, 2 * HD), BF),
            pltpu.VMEM((EX, 32, 2 * HD), BF),
            pltpu.VMEM((2 * GROUP, HD), jnp.int32),
            dma((8,)),
            dma((EX,)),
            dma((EX,)),
            dma((EX,)),
            dma((EX,)),
            dma((EX,)),
            dma((EX,)),
            dma((2, 8)),
            dma((2, 8)),
            dma((2, 8)),
            dma((2, 8)),
            dma((2, 8)),
            dma((2, 8)),
            dma((2, 20)),
            dma((2, EX)),
            dma((2, EX)),
            dma((2, EX)),
            dma((2, TP)),
            dma((2, TP)),
            dma((2, TP)),
            dma((2, TP)),
        ],
        compiler_params=pltpu.CompilerParams(
            collective_id=0, has_side_effects=True, vmem_limit_bytes=56 * 2**20
        ),
    )(
        senders,
        receivers,
        donors.T,
        norm_gain,
        corrupt_heads[0, 0],
        clean_heads[0, 0],
        out_weight[0],
        value_weight[0].T,
        residual[0, 0],
        clean_values[0, 0],
        queries[0, 0],
        key_vectors[0, 0],
    )
    return attended.reshape(1, 1, ROWS, -1)


def solution(mesh):
    return jax.shard_map(
        per_device,
        mesh=mesh,
        in_specs=(
            P("section", "ex", None, "tp"),
            P("section", "ex", None, "tp"),
            P("ex", None),
            P("section", "tp"),
            P("section", "tp", "ex"),
            P("section", "ex", None, "tp"),
            P("section", "tp"),
            P("section", "tp", "ex"),
            P("section", "ex", None, "tp"),
            P("section", "ex", None, "tp"),
            P("section", "ex", None, "tp"),
            P("section", "tp"),
        ),
        out_specs=P("section", "ex", None, "tp"),
        check_vma=False,
    )
```

```python
import math

import jax
import jax.numpy as jnp
from jax import lax
from jax.experimental import pallas as pl
from jax.experimental.pallas import tpu as pltpu
from jax.sharding import PartitionSpec as P

D = 8192
HD = 128
GROUP = 4
SEC = 4
EX = 16
TP = 4
ROWS = 512
HALF = 256
BF = jnp.bfloat16
F32 = jnp.float32
MESH = pl.DeviceIdType.MESH
CHIPS = EX // 2


def dot_nt(a, b):
    return lax.dot_general(a, b, (((1,), (1,)), ((), ())), preferred_element_type=F32)


def remote(src, dst, send, recv, device):
    return pltpu.make_async_remote_copy(
        src_ref=src,
        dst_ref=dst,
        send_sem=send,
        recv_sem=recv,
        device_id=device,
        device_id_type=MESH,
    )


def kernel(
    senders,
    receivers,
    donors,
    gain,
    corrupt_hbm,
    clean_hbm,
    weight_hbm,
    value_weight_hbm,
    residual_hbm,
    clean_values_hbm,
    queries_hbm,
    keys_hbm,
    out,
    arrived,
    patched,
    returned,
    weights,
    value_weights,
    differences,
    total,
    carried_out,
    carried_in,
    scaled,
    values_out,
    values_in,
    squares_out,
    squares_in,
    values,
    probabilities,
    residual,
    clean_values,
    queries,
    keys,
    corrupt_all,
    clean_all,
    weight_all,
    corrupt,
    clean,
    weight,
    flags,
    local_sem,
    patch_send,
    patch_recv,
    back_send,
    back_recv,
    piece_send,
    piece_recv,
    up_send,
    up_recv,
    down_send,
    down_recv,
    side_send,
    side_recv,
    diff_send,
    diff_recv,
    carry_send,
    carry_recv,
    value_send,
    value_recv,
    square_send,
    square_recv,
):
    sec = lax.axis_index("section")
    ex = lax.axis_index("ex")
    tp = lax.axis_index("tp")
    chip = ex // 2
    core = lax.rem(ex, 2)
    mine = TP * sec + tp
    group = SEC * tp + sec

    loads = [
        pltpu.make_async_copy(queries_hbm, queries, local_sem.at[0]),
        pltpu.make_async_copy(keys_hbm, keys, local_sem.at[1]),
        pltpu.make_async_copy(residual_hbm, residual, local_sem.at[2]),
        pltpu.make_async_copy(clean_values_hbm, clean_values, local_sem.at[3]),
        pltpu.make_async_copy(clean_hbm, clean_all, local_sem.at[4]),
    ]
    first_loads = [
        pltpu.make_async_copy(corrupt_hbm, corrupt_all, local_sem.at[5]),
        pltpu.make_async_copy(weight_hbm, weight_all, local_sem.at[6]),
        pltpu.make_async_copy(value_weight_hbm, value_weights.at[ex], local_sem.at[7]),
    ]
    for load in first_loads:
        load.start()

    barrier = pltpu.get_barrier_semaphore()

    @pl.loop(1, EX)
    def _(i):
        pl.semaphore_signal(
            barrier, inc=1, device_id={"ex": lax.rem(ex + i, EX)}, device_id_type=MESH
        )

    def plane_peer(i):
        other = lax.rem(mine + i, EX)
        return other // TP, lax.rem(other, TP)

    @pl.loop(1, EX)
    def _(i):
        s, t = plane_peer(i)
        pl.semaphore_signal(
            barrier, inc=1, device_id={"section": s, "tp": t}, device_id_type=MESH
        )

    heads_here = 2 * GROUP
    feature = lax.broadcasted_iota(jnp.int32, (heads_here * HD, HD), 0)
    lane = lax.broadcasted_iota(jnp.int32, (heads_here * HD, HD), 1)
    picks = []
    for i in (0, 1):
        head = senders[:, i : i + 1] - heads_here * tp
        picks.append((feature - lane == head * HD).astype(F32).astype(BF))
    pick = jnp.concatenate(picks, axis=1)
    first_loads[0].wait()
    corrupt[...] = (
        jnp.dot(corrupt_all[...], pick, preferred_element_type=F32)
        .astype(BF)
        .reshape(EX, ROWS // EX, 2 * HD)
    )

    pl.semaphore_wait(barrier, 2 * (EX - 1))

    @pl.loop(1, EX)
    def _(i):
        other = lax.rem(ex + i, EX)
        remote(
            corrupt.at[other], arrived.at[ex], patch_send.at[i], patch_recv.at[ex], {"ex": other}
        ).start()

    arrived[ex] = corrupt[ex]
    first_loads[1].wait()
    weight[...] = (
        lax.dot_general(
            weight_all[...], pick, (((0,), (0,)), ((), ())), preferred_element_type=F32
        )
        .astype(BF)
        .reshape(EX, ROWS // EX, 2 * HD)
    )

    @pl.loop(1, EX)
    def _(i):
        s, t = plane_peer(i)
        remote(
            weight.at[SEC * t + s],
            weights.at[ex, mine],
            piece_send.at[i],
            piece_recv.at[mine],
            {"section": s, "tp": t},
        ).start()

    weights[ex, mine] = weight[group]
    for load in loads:
        load.start()
    first_loads[2].wait()

    ring_up = 2 * lax.rem(chip + 1, CHIPS) + core
    ring_down = 2 * lax.rem(chip + CHIPS - 1, CHIPS) + core
    ring_side = 2 * chip + 1 - core

    def ring_copy(which, buffer, upward, origin, part, step):
        middle = buffer.shape[1] // 2
        ref = buffer.at[origin, pl.ds(part * middle, middle)]
        send, recv = (up_send, up_recv) if upward else (down_send, down_recv)
        index = 2 * step + part
        return remote(
            ref,
            ref,
            send.at[which, index],
            recv.at[which, index],
            {"ex": ring_up if upward else ring_down},
        )

    def to_side(which, buffer, origin, slot):
        ref = buffer.at[origin]
        remote(
            ref, ref, side_send.at[which, slot], side_recv.at[which, slot], {"ex": ring_side}
        ).start()

    def ring_start(which, buffer):
        for part in (0, 1):
            ring_copy(which, buffer, True, ex, part, 0).start()
            ring_copy(which, buffer, False, ex, part, 0).start()
        to_side(which, buffer, ex, 0)

    def ring_relay(which, buffer, step):
        above = 2 * lax.rem(chip + CHIPS - step, CHIPS) + core
        below = 2 * lax.rem(chip + step, CHIPS) + core
        for part in (0, 1):
            if step < 4 or part == 0:
                ring_copy(which, buffer, True, above, part, step - 1).wait_recv()
            if step < 3 or (step == 3 and part == 0):
                ring_copy(which, buffer, True, above, part, step).start()
            if step < 4 or part == 1:
                ring_copy(which, buffer, False, below, part, step - 1).wait_recv()
            if step < 3 or (step == 3 and part == 1):
                ring_copy(which, buffer, False, below, part, step).start()
        to_side(which, buffer, above, step)
        if step < 4:
            to_side(which, buffer, below, 4 + step)

    def ring_finish(which, buffer):
        side = 2 * chip + 1 - core
        for step in range(8):
            shift = CHIPS - step if step < 5 else step - 4
            block = buffer.at[2 * lax.rem(chip + shift, CHIPS) + 1 - core]
            remote(
                block, block, side_send.at[which, step], side_recv.at[which, step], {"ex": side}
            ).wait_recv()

    def ring_drain(which, buffer):
        for step in range(4):
            for part in (0, 1):
                if step < 3 or part == 0:
                    ring_copy(which, buffer, True, ex, part, step).wait_send()
                if step < 3 or part == 1:
                    ring_copy(which, buffer, False, ex, part, step).wait_send()
        block = buffer.at[ex]
        for slot in range(8):
            remote(
                block, block, side_send.at[which, slot], side_recv.at[which, slot], {"ex": ring_side}
            ).wait_send()

    def softmax(scores):
        exponent = jnp.exp(scores - jnp.max(scores, axis=-1, keepdims=True))
        return (exponent / jnp.sum(exponent, axis=-1, keepdims=True)).astype(BF)

    def weigh_heads(low, high):
        @pl.loop(low, high)
        def _(h):
            lanes = pl.ds(pl.multiple_of(h * HD, HD), HD)
            shared = pl.ds(pl.multiple_of(h // GROUP * HD, HD), HD)
            for half in (0, 1):
                length = HALF * (half + 1)
                scores = dot_nt(
                    queries[half * HALF : (half + 1) * HALF, lanes], keys[:length, shared]
                ) * (1.0 / math.sqrt(HD))
                row = lax.broadcasted_iota(jnp.int32, scores.shape, 0) + half * HALF
                column = lax.broadcasted_iota(jnp.int32, scores.shape, 1)
                scores = jnp.where(row >= column, scores, -jnp.inf)
                probabilities[h, half * HALF : (half + 1) * HALF, :length] = softmax(scores)

    block = ROWS // EX
    same = lax.broadcasted_iota(jnp.int32, (block, block), 0) == lax.broadcasted_iota(
        jnp.int32, (block, block), 1
    )
    donor = dot_nt(same.astype(F32).astype(BF), donors[...].astype(F32).astype(BF))
    row = lax.broadcasted_iota(jnp.int32, (block, ROWS), 0)
    column = lax.broadcasted_iota(jnp.int32, (block, ROWS), 1)
    offset = (column - row).astype(F32)
    onehot = jnp.concatenate(
        [
            (offset == donor[:, e : e + 1] * block).astype(F32).astype(BF)
            for e in range(EX)
        ],
        axis=0,
    )

    @pl.loop(1, EX)
    def _(i):
        other = lax.rem(ex + i, EX)
        remote(
            arrived.at[other], arrived.at[other], patch_send.at[i], patch_recv.at[other], {"ex": other}
        ).wait_recv()

    moved = jnp.dot(
        onehot, arrived[...].reshape(ROWS, 2 * HD), preferred_element_type=F32
    ).astype(BF)
    patched[...] = moved.reshape(EX, ROWS // EX, 2 * HD)

    @pl.loop(1, EX)
    def _(i):
        other = lax.rem(ex + i, EX)
        remote(
            patched.at[other], returned.at[ex], back_send.at[i], back_recv.at[ex], {"ex": other}
        ).start()

    returned[ex] = patched[ex]

    @pl.loop(1, EX)
    def _(i):
        other = lax.rem(mine + i, EX)
        remote(
            weights.at[ex, other],
            weights.at[ex, other],
            piece_send.at[i],
            piece_recv.at[other],
            {"ex": ex},
        ).wait_recv()

    ring_start(0, weights)
    loads[4].wait()
    clean[...] = jnp.dot(clean_all[...], pick, preferred_element_type=F32).astype(BF)
    for h in range(heads_here):
        flags[h : h + 1, :] = jnp.broadcast_to(receivers[:, h : h + 1], (1, HD))
    loads[0].wait()
    loads[1].wait()
    weigh_heads(0, 2)

    @pl.loop(1, EX)
    def _(i):
        other = lax.rem(ex + i, EX)
        remote(
            returned.at[other],
            returned.at[other],
            back_send.at[i],
            back_recv.at[other],
            {"ex": other},
        ).wait_recv()

    change = returned[...].reshape(ROWS, 2 * HD).astype(F32) - clean[...].astype(F32)
    differences[0, mine] = change[:HALF].astype(BF)
    differences[1, mine] = change[HALF:].astype(BF)

    axes = (("tp", "section"), ("section", "tp"))
    places = ((tp, sec), (sec, tp))

    def block_of(half, first, second):
        first, second = lax.rem(first + 8, 4), lax.rem(second + 8, 4)
        return TP * second + first if half == 0 else TP * first + second

    def difference_send(half, ref, block, axis, step, slot):
        here = sec if axis == "section" else tp
        remote(
            ref,
            ref,
            diff_send.at[half, slot],
            diff_recv.at[half, block],
            {axis: lax.rem(here + step + 4, 4)},
        ).start()

    def to_neighbours(half, phase, block, slot):
        ref = differences.at[half, block]
        difference_send(half, ref, block, axes[half][phase], 1, slot)
        difference_send(half, ref, block, axes[half][phase], -1, slot + 1)

    def pass_on(half, phase, block, step, slot):
        part = pl.ds(0, HALF // 2) if step > 0 else pl.ds(HALF // 2, HALF // 2)
        ref = differences.at[half, block, part]
        difference_send(half, ref, block, axes[half][phase], step, slot)

    def difference_wait(half, block):
        ref = differences.at[half, block]
        remote(ref, ref, diff_send.at[half, 0], diff_recv.at[half, block], {"ex": ex}).wait_recv()

    def second_phase(k):
        shift = (0, -1, 1, 2)[k]
        for half in (0, 1):
            first, second = places[half]
            for step in (1, -1):
                block = block_of(half, first + shift, second - step)
                difference_wait(half, block)
                pass_on(half, 1, block, step, 12 + 2 * k + (step < 0))

    for half in (0, 1):
        to_neighbours(half, 0, mine, 0)
    for half in (0, 1):
        to_neighbours(half, 1, mine, 2)
    for half in (0, 1):
        first, second = places[half]
        for step in (1, -1):
            block = block_of(half, first - step, second)
            difference_wait(half, block)
            pass_on(half, 0, block, step, 10 + (step < 0))
            to_neighbours(half, 1, block, 4 if step > 0 else 6)
    ring_relay(0, weights, 1)
    second_phase(0)
    ring_relay(0, weights, 2)
    for half in (0, 1):
        first, second = places[half]
        block = block_of(half, first + 2, second)
        difference_wait(half, block)
        to_neighbours(half, 1, block, 8)
    second_phase(1)
    second_phase(2)
    ring_relay(0, weights, 3)
    second_phase(3)
    ring_relay(0, weights, 4)
    ring_start(1, value_weights)
    ring_finish(0, weights)

    def carry(half):
        @pl.loop(0, SEC)
        def _(r):
            for t in range(TP):
                block = TP * r + t
                opposite = lax.rem(sec + 2, SEC) if half == 0 else lax.rem(tp + 2, TP)

                @pl.when((r if half == 0 else t) == opposite)
                def _():
                    difference_wait(half, block)

            term = dot_nt(differences[half, TP * r], weights[:, TP * r].reshape(ROWS, 2 * HD))
            for t in range(1, TP):
                term += dot_nt(
                    differences[half, TP * r + t], weights[:, TP * r + t].reshape(ROWS, 2 * HD)
                )

            @pl.when(r == 0)
            def _():
                total[...] = term

            @pl.when(r > 0)
            def _():
                total[...] += term

            rounded = total[...].astype(BF)
            for t in range(TP):
                carried_out[half, r, t] = rounded[:, t * HD : (t + 1) * HD]
            for i in range(TP):
                owner = lax.rem(tp + i, TP)
                here = jnp.logical_and(r == sec, owner == tp)

                @pl.when(here)
                def _():
                    carried_in[half, group] = carried_out[half, r, owner]

                @pl.when(jnp.logical_not(here))
                def _():
                    remote(
                        carried_out.at[half, r, owner],
                        carried_in.at[half, group],
                        carry_send.at[half, TP * r + owner],
                        carry_recv.at[half, group],
                        {"section": r, "tp": owner},
                    ).start()

    carry(0)
    ring_relay(1, value_weights, 1)
    carry(1)
    ring_relay(1, value_weights, 2)
    weigh_heads(2, 4)
    ring_relay(1, value_weights, 3)
    weigh_heads(4, 6)
    ring_relay(1, value_weights, 4)
    @pl.loop(1, EX)
    def _(i):
        remote(corrupt.at[0], arrived.at[0], patch_send.at[i], patch_recv.at[0], {"ex": 0}).wait_send()
        remote(patched.at[0], returned.at[0], back_send.at[i], back_recv.at[0], {"ex": 0}).wait_send()
        remote(
            weight.at[0], weights.at[0, 0], piece_send.at[i], piece_recv.at[0], {"ex": 0}
        ).wait_send()

    ring_drain(0, weights)
    for half in (0, 1):

        @pl.loop(0, 10)
        def _(i):
            ref = differences.at[half, 0]
            remote(ref, ref, diff_send.at[half, i], diff_recv.at[half, 0], {"ex": 0}).wait_send()
            ref = differences.at[half, 0, pl.ds(0, HALF // 2)]
            remote(
                ref, ref, diff_send.at[half, 10 + i], diff_recv.at[half, 0], {"ex": 0}
            ).wait_send()

    weigh_heads(6, 8)
    ring_finish(1, value_weights)
    loads[2].wait()
    loads[3].wait()

    source = lax.broadcasted_iota(jnp.int32, (ROWS, ROWS), 0)
    column = lax.broadcasted_iota(jnp.int32, (ROWS, ROWS), 1)
    place = source // 32 % 4 * 128 + source // 128 * 32 + source % 32
    order = (place == column).astype(F32).astype(BF)

    def finish_stream(half):
        rows = slice(half * HALF, (half + 1) * HALF)

        @pl.loop(1, EX)
        def _(i):
            other = lax.rem(group + i, EX)
            remote(
                carried_in.at[half, other],
                carried_in.at[half, other],
                carry_send.at[half, 0],
                carry_recv.at[half, other],
                {"ex": ex},
            ).wait_recv()

        square = jnp.zeros((HALF, HD), F32)
        for g in range(4):
            pieces = jnp.concatenate([carried_in[half, 4 * g + q] for q in range(4)], axis=1)
            ordered = jnp.dot(pieces, order, preferred_element_type=F32)
            for j in range(4):
                lanes = slice(j * ROWS + g * HD, j * ROWS + (g + 1) * HD)
                stream = residual[rows, lanes].astype(F32) + ordered[:, j * HD : (j + 1) * HD]
                square += stream * stream
                scaled[rows, lanes] = (stream * gain[:, lanes].astype(F32)).astype(BF)
        sums = jnp.broadcast_to(jnp.sum(square, axis=1, keepdims=True), (HALF, HD))
        squares_out[half] = jnp.transpose(sums)[:8]
        squares_in[half, tp] = squares_out[half]
        for i in range(1, TP):
            other = lax.rem(tp + i, TP)
            remote(
                squares_out.at[half],
                squares_in.at[half, tp],
                square_send.at[half, i],
                square_recv.at[half, tp],
                {"tp": other},
            ).start()

        @pl.loop(1, TP + 1)
        def _(i):
            other = lax.rem(tp + i, TP)
            columns = value_weights[pl.ds(4 * other, 4)].reshape(2 * HD, SEC * ROWS)
            values_out[half, other] = dot_nt(scaled[rows, :], columns).astype(BF)

            @pl.when(i < TP)
            def _():
                remote(
                    values_out.at[half, other],
                    values_in.at[half, tp],
                    value_send.at[half, other],
                    value_recv.at[half, tp],
                    {"tp": other},
                ).start()

        values_in[half, tp] = values_out[half, tp]

    def attend(half):
        rows = slice(half * HALF, (half + 1) * HALF)
        for i in range(1, TP):
            other = lax.rem(tp + i, TP)
            remote(
                values_in.at[half, other],
                values_in.at[half, other],
                value_send.at[half, 0],
                value_recv.at[half, other],
                {"ex": ex},
            ).wait_recv()
            remote(
                squares_in.at[half, other],
                squares_in.at[half, other],
                square_send.at[half, 0],
                square_recv.at[half, other],
                {"ex": ex},
            ).wait_recv()
        squares = (squares_in[half, 0] + squares_in[half, 1]) + (
            squares_in[half, 2] + squares_in[half, 3]
        )
        scale = lax.rsqrt(squares / D + 1e-05)
        scale = jnp.transpose(jnp.concatenate([scale] * 16, axis=0))
        for g in (0, 1):
            lanes = slice(g * HD, (g + 1) * HD)
            summed = values_in[half, 0, :, lanes].astype(F32)
            for t in range(1, TP):
                summed += values_in[half, t, :, lanes].astype(F32)
            values[rows, lanes] = (summed * scale).astype(BF)
        length = HALF * (half + 1)

        @pl.loop(0, 2 * GROUP)
        def _(h):
            shared = pl.ds(pl.multiple_of(h // GROUP * HD, HD), HD)
            flag = jnp.broadcast_to(flags[pl.ds(h, 1), :], (length, HD)) == 1
            chosen = jnp.where(
                flag,
                values[:length, shared].astype(F32),
                clean_values[:length, shared].astype(F32),
            ).astype(BF)
            out[rows, pl.ds(pl.multiple_of(h * HD, HD), HD)] = jnp.dot(
                probabilities[h, rows, :length], chosen, preferred_element_type=F32
            ).astype(BF)

    finish_stream(0)
    finish_stream(1)
    ring_drain(1, value_weights)
    for half in (0, 1):

        @pl.loop(1, EX)
        def _(i):
            other = lax.rem(mine + i, EX)
            remote(
                carried_out.at[half, 0, 0],
                carried_in.at[half, 0],
                carry_send.at[half, other],
                carry_recv.at[half, 0],
                {"ex": 0},
            ).wait_send()

    attend(0)
    attend(1)

    for half in (0, 1):
        for i in range(1, TP):
            other = lax.rem(tp + i, TP)
            remote(
                values_out.at[half, 0],
                values_in.at[half, 0],
                value_send.at[half, other],
                value_recv.at[half, 0],
                {"ex": 0},
            ).wait_send()
            remote(
                squares_out.at[half],
                squares_in.at[half, 0],
                square_send.at[half, i],
                square_recv.at[half, 0],
                {"ex": 0},
            ).wait_send()


def per_device(
    clean_heads,
    corrupt_heads,
    donors,
    senders,
    out_weight,
    residual,
    norm_gain,
    value_weight,
    clean_values,
    queries,
    key_vectors,
    receivers,
):
    dma = pltpu.SemaphoreType.DMA
    vmem = pl.BlockSpec(memory_space=pltpu.VMEM)
    hbm = pl.BlockSpec(memory_space=pl.ANY)
    attended = pl.pallas_call(
        kernel,
        out_shape=jax.ShapeDtypeStruct((ROWS, 2 * GROUP * HD), BF),
        in_specs=[vmem] * 4 + [hbm] * 8,
        out_specs=vmem,
        scratch_shapes=[
            pltpu.VMEM((EX, 32, 2 * HD), BF),
            pltpu.VMEM((EX, 32, 2 * HD), BF),
            pltpu.VMEM((EX, 32, 2 * HD), BF),
            pltpu.VMEM((EX, EX, 32, 2 * HD), BF),
            pltpu.VMEM((EX, 64, SEC * ROWS), BF),
            pltpu.VMEM((2, EX, HALF, 2 * HD), BF),
            pltpu.VMEM((HALF, ROWS), F32),
            pltpu.VMEM((2, SEC, TP, HALF, HD), BF),
            pltpu.VMEM((2, EX, HALF, HD), BF),
            pltpu.VMEM((ROWS, SEC * ROWS), BF),
            pltpu.VMEM((2, TP, HALF, 2 * HD), BF),
            pltpu.VMEM((2, TP, HALF, 2 * HD), BF),
            pltpu.VMEM((2, 8, HALF), F32),
            pltpu.VMEM((2, TP, 8, HALF), F32),
            pltpu.VMEM((ROWS, 2 * HD), BF),
            pltpu.VMEM((2 * GROUP, ROWS, ROWS), BF),
            pltpu.VMEM((ROWS, SEC * ROWS), BF),
            pltpu.VMEM((ROWS, 2 * HD), BF),
            pltpu.VMEM((ROWS, 2 * GROUP * HD), BF),
            pltpu.VMEM((ROWS, 2 * HD), BF),
            pltpu.VMEM((ROWS, 8 * HD), BF),
            pltpu.VMEM((ROWS, 8 * HD), BF),
            pltpu.VMEM((8 * HD, ROWS), BF),
            pltpu.VMEM((EX, 32, 2 * HD), BF),
            pltpu.VMEM((ROWS, 2 * HD), BF),
            pltpu.VMEM((EX, 32, 2 * HD), BF),
            pltpu.VMEM((2 * GROUP, HD), jnp.int32),
            dma((8,)),
            dma((EX,)),
            dma((EX,)),
            dma((EX,)),
            dma((EX,)),
            dma((EX,)),
            dma((EX,)),
            dma((2, 8)),
            dma((2, 8)),
            dma((2, 8)),
            dma((2, 8)),
            dma((2, 8)),
            dma((2, 8)),
            dma((2, 20)),
            dma((2, EX)),
            dma((2, EX)),
            dma((2, EX)),
            dma((2, TP)),
            dma((2, TP)),
            dma((2, TP)),
            dma((2, TP)),
        ],
        compiler_params=pltpu.CompilerParams(
            collective_id=0, has_side_effects=True, vmem_limit_bytes=56 * 2**20
        ),
    )(
        senders,
        receivers,
        donors.T,
        norm_gain,
        corrupt_heads[0, 0],
        clean_heads[0, 0],
        out_weight[0],
        value_weight[0].T,
        residual[0, 0],
        clean_values[0, 0],
        queries[0, 0],
        key_vectors[0, 0],
    )
    return attended.reshape(1, 1, ROWS, -1)


def solution(mesh):
    return jax.shard_map(
        per_device,
        mesh=mesh,
        in_specs=(
            P("section", "ex", None, "tp"),
            P("section", "ex", None, "tp"),
            P("ex", None),
            P("section", "tp"),
            P("section", "tp", "ex"),
            P("section", "ex", None, "tp"),
            P("section", "tp"),
            P("section", "tp", "ex"),
            P("section", "ex", None, "tp"),
            P("section", "ex", None, "tp"),
            P("section", "ex", None, "tp"),
            P("section", "tp"),
        ),
        out_specs=P("section", "ex", None, "tp"),
        check_vma=False,
    )
```
